512 devices in a mesh: grp: 16 (over y, core), dev: 32 (over x, z).
Axes of the slice: x: 4, y: 8, z: 8, core: 2. Of those that a mesh axis runs over, the one named last changes fastest.
Arguments:
- pixels: bfloat16 [256, 2048, 256], P('grp', 'dev'), may hold values from -16 to 16
- offsets: float32 [256, 2048], P('grp', 'dev'), may hold values from -1 to 1
- first_weights: bfloat16 [3, 256, 256], replicated, may hold values from -0.21875 to 0.21875
- second_weights: bfloat16 [3, 256, 256], replicated, may hold values from -0.21875 to 0.21875
- cotangent: bfloat16 [128, 1024, 256], P('grp', 'dev'), may hold values from -24 to 24
Outputs:
- grad_pixels: bfloat16 [256, 2048, 256], P('grp', 'dev')
- grad_first: float32 [3, 256, 256], replicated
- grad_second: float32 [3, 256, 256], replicated
- level_out: bfloat16 [128, 1024, 256], P('grp', 'dev')
The draws below stay inside these ranges and needn't reach their ends.
All inputs are finite; a program needn't handle non-finite values.
Results may differ from the reference program's by a relative error of at most 0.01.
Values may be sent and summed in bfloat16 or wider, within the bound.
No kernel may reach another device: no remote copies, remote signals or barrier semaphores. Data moves between devices by JAX's collectives and lax.ppermute only.
A program may use at most 64 MiB of HBM per device.

```python
import math
import jax
import jax.numpy as jnp
from jax import lax

F = 256
ORDERS = 3
NX = 256
NY = 2048
PX = 128
PY = 1024


def draw_pixels(key, part):
    base_key = jax.random.fold_in(key, 11)
    value_key = jax.random.fold_in(base_key, 1)
    scale_key = jax.random.fold_in(base_key, 2)
    scales = jnp.exp(jax.random.uniform(scale_key, (F,), jnp.float32, math.log(0.3), math.log(3.0)))
    values = jax.random.normal(value_key, (NX, NY, F), jnp.float32) * scales
    return jnp.clip(values, -16.0, 16.0).astype(jnp.bfloat16)


def levels(key, extent, cuts, least, largest):
    def one(dim, shards_of):
        steps = jax.random.uniform(jax.random.fold_in(jax.random.fold_in(key, 6), dim), (shards_of,), jnp.float32, least / len(cuts), largest / len(cuts))
        return jnp.repeat(jnp.exp(steps), extent[dim] // shards_of).reshape((-1,) + (1,) * (len(extent) - dim - 1))

    gain = one(*cuts[0])
    for cut in cuts[1:]:
        gain = gain * one(*cut)
    return gain


def gaussian(own_key, dims, width, bound, shards=(), held_as=jnp.bfloat16):
    level = levels(own_key, dims, shards, -0.22, 0.18) if shards else 1.0
    entries = jax.random.normal(own_key, dims, jnp.float32) * width * level
    return jnp.minimum(jnp.maximum(entries, -bound), bound).astype(held_as)


def setup_inputs(seed: int = 0) -> dict:
    keys = jax.random.split(jax.random.key(seed), 6)
    pixels = draw_pixels(jax.random.fold_in(keys[5], 71), 0)
    offsets = jnp.clip(jax.random.uniform(keys[1], (NX, NY), jnp.float32, -1.0, 1.0) * levels(keys[1], (NX, NY), ((0, 16), (1, 32)), -0.4, 0.0), -1.0, 1.0)
    first_weights = gaussian(keys[2], (ORDERS, F, F), (ORDERS * F) ** -0.5, 0.21875)
    second_weights = gaussian(keys[3], (ORDERS, F, F), (ORDERS * F) ** -0.5, 0.21875)
    cotangent = gaussian(keys[4], (PX, PY, F), 4.0, 24.0, ((0, 16), (1, 32)))
    return dict(pixels=pixels, offsets=offsets, first_weights=first_weights, second_weights=second_weights, cotangent=cotangent)


NEIGHBOUR_STEPS = ((-1, 0, 1.0), (1, 0, 1.0), (0, -1, 1.0), (0, 1, 1.0), (-1, -1, 0.5), (-1, 1, 0.5), (1, -1, 0.5), (1, 1, 0.5))

def graph_parts(offsets):
    height, breadth = offsets.shape
    padded = jnp.pad(offsets, 1)
    inside = jnp.pad(jnp.ones_like(offsets), 1)
    weights = []
    degree = jnp.zeros_like(offsets)
    for row_step, col_step, coupling in NEIGHBOUR_STEPS:
        neighbour = padded[1 + row_step:1 + row_step + height, 1 + col_step:1 + col_step + breadth]
        present = inside[1 + row_step:1 + row_step + height, 1 + col_step:1 + col_step + breadth]
        weight = coupling * present * jnp.exp(-(offsets - neighbour) * (offsets - neighbour))
        weights.append(weight)
        degree = degree + weight
    return (weights, lax.rsqrt(degree))

def apply_operator(values, weights, inverse_root):
    height, breadth = inverse_root.shape
    scaled = inverse_root[:, :, None] * values.astype(jnp.float32)
    padded = jnp.pad(scaled, ((1, 1), (1, 1), (0, 0)))
    summed = jnp.zeros(scaled.shape, jnp.float32)
    for (row_step, col_step, coupling), weight in zip(NEIGHBOUR_STEPS, weights):
        summed = summed + weight[:, :, None] * padded[1 + row_step:1 + row_step + height, 1 + col_step:1 + col_step + breadth, :]
    return -inverse_root[:, :, None] * summed

def chebyshev(values, graph_data):
    first_term = apply_operator(values, *graph_data).astype(jnp.bfloat16)
    second = (2.0 * apply_operator(first_term, *graph_data) - values.astype(jnp.float32)).astype(jnp.bfloat16)
    return jnp.concatenate([values, first_term, second], axis=-1)

def project_back(inputs, weights, order_index):
    flattened = inputs.reshape(-1, inputs.shape[-1])
    result = jnp.dot(flattened, weights[order_index].T, preferred_element_type=jnp.float32)
    return result.reshape(inputs.shape[:-1] + (weights.shape[2],))

def backward_terms(cotangent, weights, graph_data):
    top_term = project_back(cotangent, weights, 2).astype(jnp.bfloat16)
    middle = (project_back(cotangent, weights, 1) + 2.0 * apply_operator(top_term, *graph_data)).astype(jnp.bfloat16)
    return project_back(cotangent, weights, 0) - top_term.astype(jnp.float32) + apply_operator(middle, *graph_data)

def reference(pixels, offsets, first_weights, second_weights, cotangent):
    features = ORDERS * F
    fine_graph = graph_parts(offsets)
    pooled_offsets = offsets.reshape(PX, 2, PY, 2).mean(axis=(1, 3))
    pooled_graph = graph_parts(pooled_offsets)
    fine_terms = chebyshev(pixels, fine_graph)
    activation = jnp.dot(fine_terms.reshape(-1, features), first_weights.reshape(features, F), preferred_element_type=jnp.float32).reshape(NX, NY, F)
    hidden = jax.nn.silu(activation)
    pooled = hidden.reshape(PX, 2, PY, 2, F).mean(axis=(1, 3)).astype(jnp.bfloat16)
    pooled_terms = chebyshev(pooled, pooled_graph)
    level_out = jnp.dot(pooled_terms.reshape(-1, features), second_weights.reshape(features, F), preferred_element_type=jnp.float32).astype(jnp.bfloat16).reshape(PX, PY, F)
    second_sum = jnp.dot(pooled_terms.reshape(-1, features).T, cotangent.reshape(-1, F), preferred_element_type=jnp.float32).reshape(ORDERS, F, F)
    pooled_grad = backward_terms(cotangent, second_weights, pooled_graph)
    spread = jnp.broadcast_to((0.25 * pooled_grad)[:, None, :, None, :], (PX, 2, PY, 2, F)).reshape(NX, NY, F)
    sigmoid = jax.nn.sigmoid(activation)
    slope_term = sigmoid * (1.0 + activation * (1.0 - sigmoid))
    act_grad = (spread * slope_term).astype(jnp.bfloat16)
    first_sum = jnp.dot(fine_terms.reshape(-1, features).T, act_grad.reshape(-1, F), preferred_element_type=jnp.float32).reshape(ORDERS, F, F)
    grad_pixels = backward_terms(act_grad, first_weights, fine_graph).astype(jnp.bfloat16)
    square_sum = jnp.sum(first_sum * first_sum) + jnp.sum(second_sum * second_sum)
    factor = jnp.minimum(1.0, 2.0 * F * lax.rsqrt(square_sum + 1e-06))
    return (grad_pixels, first_sum * factor, second_sum * factor, level_out)
```

```python
import functools

import jax
import jax.numpy as jnp
from jax import lax
from jax.experimental import pallas as pl
from jax.experimental.pallas import tpu as pltpu
from jax.sharding import Mesh
from jax.sharding import PartitionSpec as P

GRP = ("grp_0", "grp_1")
DEV = ("dev_0", "dev_1")
EVERY = GRP + DEV
BF = jnp.bfloat16
F32 = jnp.float32

R, C, F = 16, 64, 256
PR, PC = R // 2, C // 2
HR, HC = 6, 8
ER, EC = R + 2 * HR, C + 2 * HC
QR, QC = PR + 6, PC + 8
OR = R + 16

SIDES = ((-1, 0), (1, 0), (0, -1), (0, 1), (-1, -1), (-1, 1), (1, -1), (1, 1))
STEPS = (
    (-1, 0, 1.0),
    (1, 0, 1.0),
    (0, -1, 1.0),
    (0, 1, 1.0),
    (-1, -1, 0.5),
    (-1, 1, 0.5),
    (1, -1, 0.5),
    (1, 1, 0.5),
)


def mm(a, b):
    return lax.dot_general(a, b, (((1,), (0,)), ((), ())), preferred_element_type=F32)


def mm_nt(a, b):
    return lax.dot_general(a, b, (((1,), (1,)), ((), ())), preferred_element_type=F32)


def mm_tn(a, b):
    return lax.dot_general(a, b, (((0,), (0,)), ((), ())), preferred_element_type=F32)


def px_rows(di):
    return {-1: (0, HR), 1: (R - HR, HR), 0: (0, R)}[di]


def ct_rows(di):
    return {-1: (0, 3), 1: (PR - 3, 3), 0: (0, PR)}[di]


def off_rows(di):
    return {-1: (0, 8), 1: (R - 8, 8), 0: (0, R)}[di]


def message_parts(di, dj):
    px = px_rows(di)[1] * (HC if dj else C)
    ct = ct_rows(di)[1] * (8 if dj else PC)
    ct += -ct % 16
    off = 48 if di == 0 else 32
    return px, px + ct, px + ct + off


def rolled(x, shift, axis):
    return pltpu.roll(x, shift % x.shape[axis], axis)


def pack_kernel(px_ref, ct_ref, off_ref, *rest):
    outs, wide = rest[:8], rest[8]
    wide[...] = jnp.zeros_like(wide)
    wide[:, 0:C] = off_ref[...]
    lane = lax.broadcasted_iota(jnp.int32, (R, 128), 1)
    for (di, dj), out in zip(SIDES, outs):
        ct_at, off_at, _ = message_parts(di, dj)
        first, count = px_rows(di)
        if dj == 0:
            out[0 : count * C, :] = px_ref[first * C : (first + count) * C, :]
        else:
            start = 0 if dj < 0 else C - 16
            half = slice(0, 8) if dj < 0 else slice(8, 16)
            for r in range(0, count, 2):
                tiles = []
                for k in (0, 1):
                    at = (first + r + k) * C + start
                    tiles.append(px_ref[at : at + 16, :].astype(F32)[half])
                out[r * 8 : r * 8 + 16, :] = jnp.concatenate(tiles, 0).astype(BF)
        first, count = ct_rows(di)
        if dj == 0:
            out[ct_at : ct_at + count * PC, :] = ct_ref[first * PC : (first + count) * PC, :]
        else:
            start = 0 if dj < 0 else PC - 16
            half = slice(0, 8) if dj < 0 else slice(8, 16)
            for r in range(0, count, 2):
                tiles = []
                for k in (0, 1):
                    if r + k < count:
                        at = (first + r + k) * PC + start
                        tiles.append(ct_ref[at : at + 16, :].astype(F32)[half])
                    else:
                        tiles.append(jnp.zeros((8, F), F32))
                at = ct_at + r * 8
                out[at : at + 16, :] = jnp.concatenate(tiles, 0).astype(BF)
        first, count = off_rows(di)
        part = wide[first : first + count, :]
        lanes = lane[0:count]
        if dj < 0:
            part = jnp.where(lanes < HC, part, 0.0)
        elif dj > 0:
            part = jnp.where(lanes < HC, rolled(part, HC - C, 1), 0.0)
        high = part.astype(BF).astype(F32)
        left = part - high
        middle = left.astype(BF).astype(F32)
        low = left - middle
        if di == 0:
            packed = jnp.concatenate([high, middle, low], 0)
        else:
            packed = jnp.concatenate([high, middle, low, jnp.zeros_like(low)], 0)
        packed = jnp.concatenate([packed, jnp.zeros_like(packed)], 1)
        out[off_at : off_at + packed.shape[0], :] = packed.astype(BF)


def packed_messages(pixels, cotangent, offsets):
    shapes = [jax.ShapeDtypeStruct((message_parts(*side)[2], F), BF) for side in SIDES]
    return pl.pallas_call(
        pack_kernel,
        out_shape=shapes,
        scratch_shapes=[pltpu.VMEM((R, 128), F32)],
        name="pack",
    )(pixels, cotangent, offsets)


def exchanged(messages):
    rows = lax.axis_size(GRP)
    cols = lax.axis_size(DEV)
    got = []
    for di, dj in SIDES:
        pairs = []
        for i in range(rows):
            for j in range(cols):
                if 0 <= i + di < rows and 0 <= j + dj < cols:
                    pairs.append(((i + di) * cols + j + dj, i * cols + j))
        got.append(lax.ppermute(messages[SIDES.index((-di, -dj))], EVERY, pairs))
    return got


def inverse_roots(h, inside):
    degree = jnp.zeros_like(h)
    for row_step, col_step, coupling in STEPS:
        other = rolled(rolled(h, -row_step, 0), -col_step, 1)
        present = rolled(rolled(inside, -row_step, 0), -col_step, 1)
        degree = degree + coupling * present * jnp.exp(-(h - other) * (h - other))
    return lax.rsqrt(degree + 1.0 - inside) * inside


def couplings(row_gap, col_gap):
    near = jnp.abs(col_gap)
    side = jnp.where(near == 0, 1.0, jnp.where(near == 1, 0.5, 0.0))
    own = jnp.where(near == 1, 1.0, 0.0)
    return jnp.where(row_gap == 0, own, jnp.where(jnp.abs(row_gap) == 1, side, 0.0))


def fine_windows(x):
    lane = lax.broadcasted_iota(jnp.int32, x.shape, 1)
    over = rolled(x, EC, 1)
    low = jnp.where(lane < EC, rolled(x, 1, 0), over)
    high = jnp.where(lane < 2 * EC - 128, over, rolled(rolled(x, -1, 0), 2 * EC - 128, 1))
    return jnp.concatenate([low, high], 1)


def pooled_windows(x):
    lane = lax.broadcasted_iota(jnp.int32, x.shape, 1)
    rows = [rolled(rolled(x, 1 - j, 0), QC * j, 1) for j in range(6)]
    low = jnp.where(
        lane < QC,
        rows[0],
        jnp.where(lane < 2 * QC, rows[1], jnp.where(lane < 3 * QC, rows[2], rows[3])),
    )
    high = jnp.where(
        lane < 4 * QC - 128,
        rows[3],
        jnp.where(
            lane < 5 * QC - 128, rows[4], jnp.where(lane < 6 * QC - 128, rows[5], 0.0)
        ),
    )
    return jnp.concatenate([low, high], 1)


def transposed(x):
    if x.shape[0] < 128:
        x = jnp.concatenate([x, jnp.zeros((128 - x.shape[0], 128), F32)], 0)
    return x.T


def main_kernel(px_ref, ct_ref, off_ref, w1_ref, w2_ref, *rest):
    got = dict(zip(SIDES, rest[:8]))
    level_ref, sums_ref, table_ref, grad_ref = rest[8:12]
    (h_ref, hw_ref, sw_ref, pxe_ref, f1_ref, f2_ref, f1c_ref, f2c_ref, slope_ref, hid_ref,
     poolf_ref, p1f_ref, p2f_ref, ctf_ref, ptab_ref, pb_ref, p1b_ref, ctb_ref, topb_ref,
     midf_ref, midb_ref, pgf_ref, sp_ref, agc_ref, low_ref) = rest[12:]

    row0 = (lax.axis_index("grp_0") * 2 + lax.axis_index("grp_1")) * R
    col0 = (lax.axis_index("dev_0") * lax.axis_size("dev_1") + lax.axis_index("dev_1")) * C
    rows_all = lax.axis_size("grp_0") * lax.axis_size("grp_1") * R
    cols_all = lax.axis_size("dev_0") * lax.axis_size("dev_1") * C

    h_ref[...] = jnp.zeros_like(h_ref)
    h_ref[8 : 8 + R, 0:C] = off_ref[...]

    def offsets_of(side):
        ref = got[side]
        _, at, end = message_parts(*side)
        all_parts = ref[at:end, 0:128].astype(F32)
        n = R if side[0] == 0 else 8
        return all_parts[0:n] + all_parts[n : 2 * n] + all_parts[2 * n : 3 * n]

    for di, at, n in ((-1, 0, 8), (0, 8, R), (1, 8 + R, 8)):
        middle = h_ref[at : at + n, :] if di == 0 else offsets_of((di, 0))
        h_ref[at : at + n, :] = (
            offsets_of((di, -1)) + rolled(middle, HC, 1) + rolled(offsets_of((di, 1)), HC + C, 1)
        )
    h = h_ref[...]
    q = lax.broadcasted_iota(jnp.int32, (OR, 128), 0)
    c = lax.broadcasted_iota(jnp.int32, (OR, 128), 1)
    row_id = row0 - 8 + q
    col_id = col0 - HC + c
    inside = (
        (row_id >= 0) & (row_id < rows_all) & (col_id >= 0) & (col_id < cols_all) & (c < EC)
    ).astype(F32)
    s = inverse_roots(h, inside)

    pick_r = lax.broadcasted_iota(jnp.int32, (OR // 2, OR), 1) // 2
    pick_r = jnp.where(pick_r == lax.broadcasted_iota(jnp.int32, (OR // 2, OR), 0), 0.5, 0.0)
    pick_c = lax.broadcasted_iota(jnp.int32, (128, 128), 0) // 2
    pick_c = jnp.where(pick_c == lax.broadcasted_iota(jnp.int32, (128, 128), 1), 0.5, 0.0)
    ph = jnp.dot(pick_r, h, precision=lax.Precision.HIGHEST, preferred_element_type=F32)
    ph = jnp.dot(ph, pick_c, precision=lax.Precision.HIGHEST, preferred_element_type=F32)
    pq = lax.broadcasted_iota(jnp.int32, (OR // 2, 128), 0)
    pc = lax.broadcasted_iota(jnp.int32, (OR // 2, 128), 1)
    prow = row0 // 2 - 4 + pq
    pcol = col0 // 2 - 4 + pc
    pinside = (
        (prow >= 0) & (prow < rows_all // 2) & (pcol >= 0) & (pcol < cols_all // 2) & (pc < QC)
    ).astype(F32)
    ps = inverse_roots(ph, pinside)

    hw_ref[0:OR, :] = fine_windows(h)
    sw_ref[0:OR, :] = fine_windows(s)
    hw_ref[OR : OR + OR // 2, :] = pooled_windows(ph)
    sw_ref[OR : OR + OR // 2, :] = pooled_windows(ps)
    ht, st = transposed(h), transposed(s)
    pht, pst = transposed(ph), transposed(ps)
    k = lax.broadcasted_iota(jnp.int32, (EC, 256), 1)
    i = lax.broadcasted_iota(jnp.int32, (EC, 256), 0)
    block = (k >= EC).astype(jnp.int32) + (k >= 2 * EC).astype(jnp.int32)
    link = -couplings(block - 1, k - block * EC - i)
    for r in range(1, ER - 1):
        at = r + 2
        gap = ht[0:EC, at : at + 1] - hw_ref[at : at + 1, :]
        scale = st[0:EC, at : at + 1] * sw_ref[at : at + 1, :]
        table = link * jnp.exp(-gap * gap) * scale
        table_ref[(r - 1) * EC : r * EC, :] = table.astype(BF)
    k = lax.broadcasted_iota(jnp.int32, (QC, 256), 1)
    i = lax.broadcasted_iota(jnp.int32, (QC, 256), 0)
    block = sum((k >= QC * j).astype(jnp.int32) for j in range(1, 6))
    plinks = [-couplings(block - 1 - j, k - block * QC - i) for j in range(4)]
    for b in range(3):
        at = 2 + 4 * b
        for j in (0, 2):
            both = []
            for jj in (j, j + 1):
                col = at + jj
                gap = pht[0:QC, col : col + 1] - hw_ref[OR + at : OR + at + 1, :]
                scale = pst[0:QC, col : col + 1] * sw_ref[OR + at : OR + at + 1, :]
                both.append(plinks[jj] * jnp.exp(-gap * gap) * scale)
            ptab_ref[b * 160 + j * QC : b * 160 + (j + 2) * QC, :] = jnp.concatenate(both, 0).astype(BF)

    for di, at, n in ((-1, 0, HR), (0, HR, R), (1, HR + R, HR)):
        lefts, rights = got[(di, -1)], got[(di, 1)]
        middles = px_ref if di == 0 else got[(di, 0)]
        for r in range(0, n, 2):
            left = lefts[r * 8 : r * 8 + 16, :].astype(F32)
            right = rights[r * 8 : r * 8 + 16, :].astype(F32)
            middle = middles[r * C : (r + 2) * C, :].astype(F32)
            lines = [left[0:8], middle[0:C], right[0:8], left[8:16], middle[C:], right[8:16]]
            row = (at + r) * EC
            pxe_ref[row : row + 2 * EC, :] = jnp.concatenate(lines, 0).astype(BF)

    for di, at, n in ((-1, 0, 3), (0, 3, PR), (1, 3 + PR, 3)):
        lefts, rights = got[(di, -1)], got[(di, 1)]
        side_at = message_parts(di, 1)[0]
        middles = ct_ref if di == 0 else got[(di, 0)]
        mid_at = 0 if di == 0 else message_parts(di, 0)[0]
        for r in range(0, n, 2):
            left = lefts[side_at + r * 8 : side_at + r * 8 + 16, :].astype(F32)
            right = rights[side_at + r * 8 : side_at + r * 8 + 16, :].astype(F32)
            for kk in range(min(2, n - r)):
                base = (at + r + kk) * QC
                ctf_ref[base : base + 4, :] = left[kk * 8 + 4 : kk * 8 + 8]
                from_at = mid_at + (r + kk) * PC
                ctf_ref[base + 4 : base + 4 + PC, :] = middles[from_at : from_at + PC, :].astype(F32)
                ctf_ref[base + 4 + PC : base + QC, :] = right[kk * 8 : kk * 8 + 4]
    ctb_ref[...] = ctf_ref[...].astype(BF)

    def table_of(r):
        return table_ref[(r - 1) * EC : r * EC, 0 : 3 * EC]

    for r in range(1, ER - 1):
        one = mm(table_of(r), pxe_ref[(r - 1) * EC : (r + 2) * EC, :])
        f1_ref[(r - 1) * EC : r * EC, :] = one.astype(BF)
        if HR <= r < HR + R:
            f1c_ref[(r - HR) * C : (r - HR + 1) * C, :] = one[HC : HC + C].astype(BF)
    for r in range(2, ER - 2):
        two = 2.0 * mm(table_of(r), f1_ref[(r - 2) * EC : (r + 1) * EC, :])
        two = two - pxe_ref[r * EC : (r + 1) * EC, :].astype(F32)
        f2_ref[(r - 2) * EC : (r - 1) * EC, :] = two.astype(BF)
        if HR <= r < HR + R:
            f2c_ref[(r - HR) * C : (r - HR + 1) * C, :] = two[HC : HC + C].astype(BF)
    poolf_ref[...] = jnp.zeros_like(poolf_ref)
    p1f_ref[...] = jnp.zeros_like(p1f_ref)
    midf_ref[...] = jnp.zeros_like(midf_ref)
    for b in range(6):
        r = 2 + 4 * b
        act = mm(pxe_ref[r * EC : (r + 4) * EC, :], w1_ref[0])
        act = act + mm(f1_ref[(r - 1) * EC : (r + 3) * EC, :], w1_ref[1])
        act = act + mm(f2_ref[(r - 2) * EC : (r + 2) * EC, :], w1_ref[2])
        sig = 1.0 / (1.0 + jnp.exp(-act))
        slope_ref[(r - 2) * EC : (r + 2) * EC, :] = sig * (1.0 + act * (1.0 - sig))
        hid = act * sig
        for n in (0, 1):
            half = hid[:, n * 128 : (n + 1) * 128]
            ref = hid_ref.at[2 * b + n]
            ref[0:EC, :] = half[0:EC] + half[EC : 2 * EC]
            ref[EC : 2 * EC, :] = half[2 * EC : 3 * EC] + half[3 * EC : 4 * EC]
            pooled = 0.25 * (ref[pl.ds(0, EC, stride=2), :] + ref[pl.ds(1, EC, stride=2), :])
            pooled = pooled.astype(BF).astype(F32)
            poolf_ref[(1 + 2 * b) * QC : (3 + 2 * b) * QC, n * 128 : (n + 1) * 128] = pooled
    pb_ref[...] = poolf_ref[...].astype(BF)

    def ptable_of(b):
        return ptab_ref[b * 160 : (b + 1) * 160, 0 : 6 * QC]

    for b in range(3):
        one = mm(ptable_of(b), pb_ref[b * 160 : b * 160 + 6 * QC, :])
        p1f_ref[(1 + 4 * b) * QC : (5 + 4 * b) * QC, :] = one
    p1b_ref[...] = p1f_ref[...].astype(BF)
    for b in range(3):
        two = 2.0 * mm(ptable_of(b), p1b_ref[b * 160 : b * 160 + 6 * QC, :])
        lines = slice((1 + 4 * b) * QC, (5 + 4 * b) * QC)
        p2f_ref[lines, :] = two - poolf_ref[lines, :]
    own = slice(3 * QC, 11 * QC)
    terms = [poolf_ref[own, :].astype(BF), p1f_ref[own, :].astype(BF), p2f_ref[own, :].astype(BF)]
    low_ref[...] = sum(mm(term, w2_ref[n]) for n, term in enumerate(terms))
    for r in range(PR):
        level_ref[r * PC : (r + 1) * PC, :] = low_ref[r * QC + 4 : r * QC + 4 + PC, :].astype(BF)
    col = lax.broadcasted_iota(jnp.int32, (QC, F), 0)
    keep = ((col >= 4) & (col < 4 + PC)).astype(F32)
    cot_own = (ctf_ref[own, :].reshape(PR, QC, F) * keep[None]).reshape(PR * QC, F).astype(BF)
    for n, term in enumerate(terms):
        sums_ref[(3 + n) * F : (4 + n) * F, :] = mm_tn(term, cot_own).astype(sums_ref.dtype)

    cot = ctb_ref[...]
    topb_ref[...] = mm_nt(cot, w2_ref[2]).astype(BF)
    from_one = mm_nt(cot, w2_ref[1])
    for b in range(3):
        lines = slice((1 + 4 * b) * QC, (5 + 4 * b) * QC)
        mid = 2.0 * mm(ptable_of(b), topb_ref[b * 160 : b * 160 + 6 * QC, :])
        midf_ref[lines, :] = from_one[lines] + mid
    midb_ref[...] = midf_ref[...].astype(BF)
    from_zero = mm_nt(cot, w2_ref[0]) - topb_ref[...].astype(F32)
    for b in range(3):
        lines = slice((1 + 4 * b) * QC, (5 + 4 * b) * QC)
        pgf_ref[lines, :] = from_zero[lines] + mm(ptable_of(b), midb_ref[b * 160 : b * 160 + 6 * QC, :])
    for b in range(5):
        u = 2 + 2 * b
        grad = 0.25 * pgf_ref[u * QC : (u + 2) * QC, :]
        for n in (0, 1):
            ref = sp_ref.at[2 * b + n]
            ref[pl.ds(0, 2 * QC, stride=2), :] = grad[:, n * 128 : (n + 1) * 128]
            ref[pl.ds(1, 2 * QC, stride=2), :] = grad[:, n * 128 : (n + 1) * 128]
        for n in range(4):
            r = 2 * u + n
            lines = slice((n // 2) * EC, (n // 2 + 1) * EC)
            spread = jnp.concatenate([sp_ref[2 * b, lines, :], sp_ref[2 * b + 1, lines, :]], 1)
            grad_row = spread * slope_ref[(r - 2) * EC : (r - 1) * EC, :]
            grad_ref[(r - 4) * EC : (r - 3) * EC, :] = grad_row.astype(BF)
            if HR <= r < HR + R:
                agc_ref[(r - HR) * C : (r - HR + 1) * C, :] = grad_row[HC : HC + C].astype(BF)
    for n, ref in enumerate((px_ref, f1c_ref, f2c_ref)):
        sums_ref[n * F : (n + 1) * F, :] = mm_tn(ref[...], agc_ref[...]).astype(sums_ref.dtype)


def main_stage(pixels, cotangent, offsets, first_weights, second_weights, got):
    fine, pooled = ER * EC, QR * QC
    scratch = [
        ((OR, 128), F32),
        ((OR + OR // 2, 256), F32),
        ((OR + OR // 2, 256), F32),
        ((fine, F), BF),
        ((26 * EC, F), BF),
        ((24 * EC, F), BF),
        ((R * C, F), BF),
        ((R * C, F), BF),
        ((24 * EC, F), F32),
        ((12, 2 * EC, 128), F32),
        ((pooled, F), F32),
        ((pooled, F), F32),
        ((pooled, F), F32),
        ((pooled, F), F32),
        ((480, 256), BF),
        ((pooled, F), BF),
        ((pooled, F), BF),
        ((pooled, F), BF),
        ((pooled, F), BF),
        ((pooled, F), F32),
        ((pooled, F), BF),
        ((pooled, F), F32),
        ((10, 2 * EC, 128), F32),
        ((R * C, F), BF),
        ((PR * QC, F), F32),
    ]
    return pl.pallas_call(
        main_kernel,
        out_shape=[
            jax.ShapeDtypeStruct((PR * PC, F), BF),
            jax.ShapeDtypeStruct((6 * F, F), BF),
            jax.ShapeDtypeStruct((26 * EC, 256), BF),
            jax.ShapeDtypeStruct((20 * EC, F), BF),
        ],
        scratch_shapes=[pltpu.VMEM(shape, dtype) for shape, dtype in scratch],
        compiler_params=pltpu.CompilerParams(vmem_limit_bytes=56 << 20),
        name="main",
    )(pixels, cotangent, offsets, first_weights, second_weights, *got)


def tail_kernel(table_ref, grad_ref, w_ref, out_ref, top_ref, mid_ref):
    top_ref[...] = mm_nt(grad_ref[...], w_ref[2]).astype(BF)
    for b in range(9):
        r = 5 + 2 * b
        base = mm_nt(grad_ref[(r - 4) * EC : (r - 2) * EC, :], w_ref[1])
        for n in (0, 1):
            table = table_ref[(r + n - 1) * EC : (r + n) * EC, 0 : 3 * EC]
            mid = 2.0 * mm(table, top_ref[(r + n - 5) * EC : (r + n - 2) * EC, :])
            mid = base[n * EC : (n + 1) * EC] + mid
            mid_ref[(r + n - 5) * EC : (r + n - 4) * EC, :] = mid.astype(BF)
    for b in range(8):
        r = 6 + 2 * b
        base = mm_nt(grad_ref[(r - 4) * EC : (r - 2) * EC, :], w_ref[0])
        base = base - top_ref[(r - 4) * EC : (r - 2) * EC, :].astype(F32)
        for n in (0, 1):
            table = table_ref[(r + n - 1) * EC : (r + n) * EC, 0 : 3 * EC]
            line = base[n * EC : (n + 1) * EC] + mm(table, mid_ref[(r + n - 6) * EC : (r + n - 3) * EC, :])
            at = (r + n - HR) * C
            out_ref[at : at + C, :] = line[HC : HC + C].astype(BF)


def tail_stage(table, grad, first_weights):
    return pl.pallas_call(
        tail_kernel,
        out_shape=jax.ShapeDtypeStruct((R * C, F), BF),
        scratch_shapes=[pltpu.VMEM((20 * EC, F), BF), pltpu.VMEM((18 * EC, F), BF)],
        compiler_params=pltpu.CompilerParams(vmem_limit_bytes=56 << 20),
        name="tail",
    )(table, grad, first_weights)


def sum_at_owner(value, axes):
    size = lax.axis_size(axes)
    tiles = lax.all_to_all(value.reshape(size, -1, F), axes, 0, 0, tiled=True)
    return jnp.sum(tiles.astype(F32), axis=0).astype(BF)


def sent_to_all(value, axes):
    copies = jnp.broadcast_to(value, (lax.axis_size(axes), *value.shape))
    return lax.all_to_all(copies, axes, 0, 0, tiled=True).reshape(-1, F)


def total_of(value):
    stages = (("grp_1", "dev_0"), ("grp_0", "dev_1"))
    for axes in stages:
        value = sum_at_owner(value, axes)
    for axes in stages[::-1]:
        value = sent_to_all(value, axes)
    return value


def clip_kernel(sums_ref, first_ref, second_ref):
    total = jnp.zeros((8, F), F32)
    for n in range(6):
        part = sums_ref[n * F : (n + 1) * F, :].astype(F32)
        total = total + jnp.sum((part * part).reshape(F // 8, 8, F), axis=0)
    square_sum = jnp.sum(jnp.sum(total, axis=1, keepdims=True), axis=0, keepdims=True)
    factor = jnp.minimum(1.0, 2.0 * F * lax.rsqrt(square_sum + 1e-06))
    for n in range(3):
        first_ref[n] = sums_ref[n * F : (n + 1) * F, :].astype(F32) * factor
        second_ref[n] = sums_ref[(3 + n) * F : (4 + n) * F, :].astype(F32) * factor


def clipped(sums):
    shape = jax.ShapeDtypeStruct((3, F, F), F32)
    return pl.pallas_call(clip_kernel, out_shape=[shape, shape], name="clip")(sums)


def shards(pixels, offsets, first_weights, second_weights, cotangent):
    px = pixels.reshape(R * C, F)
    ct = cotangent.reshape(PR * PC, F)
    got = exchanged(packed_messages(px, ct, offsets))
    level, sums, table, grad = main_stage(px, ct, offsets, first_weights, second_weights, got)
    first, second = clipped(total_of(sums))
    grad_pixels = tail_stage(table, grad, first_weights)
    return grad_pixels.reshape(R, C, F), first, second, level.reshape(PR, PC, F)


def solution(mesh):
    finer = Mesh(mesh.devices.reshape(-1, 2, 4, mesh.devices.shape[1] // 4), EVERY)
    in_specs = (P(GRP, DEV, None), P(GRP, DEV), P(), P(), P(GRP, DEV, None))
    out_specs = (P(GRP, DEV, None), P(), P(), P(GRP, DEV, None))
    return jax.shard_map(
        shards, mesh=finer, in_specs=in_specs, out_specs=out_specs, check_vma=False
    )
```

```python
import functools

import jax
import jax.numpy as jnp
from jax import lax
from jax.experimental import pallas as pl
from jax.experimental.pallas import tpu as pltpu
from jax.sharding import Mesh
from jax.sharding import PartitionSpec as P

GRP = ("grp_0", "grp_1")
DEV = ("dev_0", "dev_1")
EVERY = GRP + DEV
BF = jnp.bfloat16
F32 = jnp.float32

R, C, F = 16, 64, 256
PR, PC = R // 2, C // 2
HR, HC = 6, 8
ER, EC = R + 2 * HR, C + 2 * HC
QR, QC = PR + 6, PC + 8
OR = R + 16

STEPS = (
    (-1, 0, 1.0),
    (1, 0, 1.0),
    (0, -1, 1.0),
    (0, 1, 1.0),
    (-1, -1, 0.5),
    (-1, 1, 0.5),
    (1, -1, 0.5),
    (1, 1, 0.5),
)


def mm(a, b):
    return lax.dot_general(a, b, (((1,), (0,)), ((), ())), preferred_element_type=F32)


def mm_nt(a, b):
    return lax.dot_general(a, b, (((1,), (1,)), ((), ())), preferred_element_type=F32)


def mm_tn(a, b):
    return lax.dot_general(a, b, (((0,), (0,)), ((), ())), preferred_element_type=F32)


ROW_CT = HR * C
ROW_OFF = ROW_CT + 3 * PC
ROW_END = ROW_OFF + 32
COL_CT = ER * HC
COL_OFF = COL_CT + 64
COL_END = COL_OFF + OR


def rolled(x, shift, axis):
    return pltpu.roll(x, shift % x.shape[axis], axis)


def in_parts(x):
    high = x.astype(BF).astype(F32)
    left = x - high
    middle = left.astype(BF).astype(F32)
    return high, middle, left - middle


def row_pack_kernel(px_ref, ct_ref, off_ref, up_ref, down_ref, wide):
    wide[...] = jnp.zeros_like(wide)
    wide[:, 0:C] = off_ref[...]
    for out, px_at, ct_at, off_at in ((up_ref, 0, 0, 0), (down_ref, R - HR, PR - 3, R - 8)):
        out[0:ROW_CT, :] = px_ref[px_at * C : (px_at + HR) * C, :]
        out[ROW_CT:ROW_OFF, :] = ct_ref[ct_at * PC : (ct_at + 3) * PC, :]
        high, middle, low = in_parts(wide[off_at : off_at + 8, :])
        packed = jnp.concatenate([high, middle, low, jnp.zeros_like(low)], 0)
        out[ROW_OFF:ROW_END, :] = jnp.concatenate([packed, jnp.zeros_like(packed)], 1).astype(BF)


def row_messages(pixels, cotangent, offsets):
    shape = jax.ShapeDtypeStruct((ROW_END, F), BF)
    return pl.pallas_call(
        row_pack_kernel,
        out_shape=[shape, shape],
        scratch_shapes=[pltpu.VMEM((R, 128), F32)],
        name="row_pack",
    )(pixels, cotangent, offsets)


def row_offsets(ref):
    parts = ref[ROW_OFF:ROW_END, 0:128].astype(F32)
    return parts[0:8] + parts[8:16] + parts[16:24]


def col_pack_kernel(px_ref, ct_ref, off_ref, above_ref, below_ref, left_ref, right_ref, wide):
    wide[...] = jnp.zeros_like(wide)
    wide[8 : 8 + R, 0:C] = off_ref[...]
    wide[0:8, :] = row_offsets(above_ref)
    wide[8 + R : OR, :] = row_offsets(below_ref)
    lane = lax.broadcasted_iota(jnp.int32, (OR, 128), 1)
    near = lax.broadcasted_iota(jnp.int32, (8, F), 0) < 4
    for out, px_at, ct_at, half in (
        (left_ref, 0, 0, slice(0, 8)),
        (right_ref, C - 16, PC - 16, slice(8, 16)),
    ):
        for first, n, ref in ((0, HR, above_ref), (HR, R, px_ref), (HR + R, HR, below_ref)):
            for r in range(0, n, 2):
                tiles = []
                for k in (r, r + 1):
                    at = k * C + px_at
                    tiles.append(ref[at : at + 16, :].astype(F32)[half])
                at = (first + r) * HC
                out[at : at + 16, :] = jnp.concatenate(tiles, 0).astype(BF)
        lines = []
        for base, n, ref in ((ROW_CT, 3, above_ref), (0, PR, ct_ref), (ROW_CT, 3, below_ref)):
            for r in range(n):
                at = base + r * PC + ct_at
                lines.append(ref[at : at + 16, :].astype(F32)[half])
        tiles = []
        for e in range(0, QR, 2):
            first, second = lines[e], lines[e + 1]
            if out is left_ref:
                second = rolled(second, 4, 0)
            else:
                first = rolled(first, 4, 0)
            tiles.append(jnp.where(near, first, second))
        tiles.append(jnp.zeros((8, F), F32))
        out[COL_CT:COL_OFF, :] = jnp.concatenate(tiles, 0).astype(BF)
        part = wide[...] if out is left_ref else rolled(wide[...], HC - C, 1)
        high, middle, low = in_parts(jnp.where(lane < HC, part, 0.0))
        packed = high + rolled(middle, HC, 1) + rolled(low, 2 * HC, 1)
        out[COL_OFF:COL_END, :] = jnp.concatenate([packed, jnp.zeros_like(packed)], 1).astype(BF)


def col_messages(pixels, cotangent, offsets, above, below):
    shape = jax.ShapeDtypeStruct((COL_END, F), BF)
    return pl.pallas_call(
        col_pack_kernel,
        out_shape=[shape, shape],
        scratch_shapes=[pltpu.VMEM((OR, 128), F32)],
        name="col_pack",
    )(pixels, cotangent, offsets, above, below)


def exchanged(first, last, axis):
    count = lax.axis_size(axis)
    forward = [(i, i + 1) for i in range(count - 1)]
    backward = [(i + 1, i) for i in range(count - 1)]
    return lax.ppermute(last, axis, forward), lax.ppermute(first, axis, backward)


def inverse_roots(h, inside):
    degree = jnp.zeros_like(h)
    for row_step, col_step, coupling in STEPS:
        other = rolled(rolled(h, -row_step, 0), -col_step, 1)
        present = rolled(rolled(inside, -row_step, 0), -col_step, 1)
        degree = degree + coupling * present * jnp.exp(-(h - other) * (h - other))
    return lax.rsqrt(degree + 1.0 - inside) * inside


def couplings(row_gap, col_gap):
    near = jnp.abs(col_gap)
    side = jnp.where(near == 0, 1.0, jnp.where(near == 1, 0.5, 0.0))
    own = jnp.where(near == 1, 1.0, 0.0)
    return jnp.where(row_gap == 0, own, jnp.where(jnp.abs(row_gap) == 1, side, 0.0))


def fine_windows(x):
    lane = lax.broadcasted_iota(jnp.int32, x.shape, 1)
    over = rolled(x, EC, 1)
    low = jnp.where(lane < EC, rolled(x, 1, 0), over)
    high = jnp.where(lane < 2 * EC - 128, over, rolled(rolled(x, -1, 0), 2 * EC - 128, 1))
    return jnp.concatenate([low, high], 1)


def pooled_windows(x):
    lane = lax.broadcasted_iota(jnp.int32, x.shape, 1)
    rows = [rolled(rolled(x, 1 - j, 0), QC * j, 1) for j in range(6)]
    low = jnp.where(
        lane < QC,
        rows[0],
        jnp.where(lane < 2 * QC, rows[1], jnp.where(lane < 3 * QC, rows[2], rows[3])),
    )
    high = jnp.where(
        lane < 4 * QC - 128,
        rows[3],
        jnp.where(
            lane < 5 * QC - 128, rows[4], jnp.where(lane < 6 * QC - 128, rows[5], 0.0)
        ),
    )
    return jnp.concatenate([low, high], 1)


def in_two(x):
    high = x.astype(BF)
    return jnp.concatenate([high, (x - high.astype(F32)).astype(BF)], 0)


def applied(table, values):
    both = mm(table, values)
    half = both.shape[0] // 2
    return both[0:half] + both[half:]


def transposed(x):
    if x.shape[0] < 128:
        x = jnp.concatenate([x, jnp.zeros((128 - x.shape[0], 128), F32)], 0)
    return x.T


def main_kernel(px_ref, ct_ref, off_ref, w1_ref, w2_ref, above_ref, below_ref, left_ref, right_ref, *rest):
    level_ref, sums_ref, table_ref, grad_ref = rest[:4]
    (h_ref, hw_ref, sw_ref, pxe_ref, f1_ref, f2_ref, f1c_ref, f2c_ref, slope_ref, hid_ref,
     poolf_ref, p1f_ref, p2f_ref, ctf_ref, ptab_ref, pb_ref, p1b_ref, ctb_ref, topb_ref,
     midf_ref, midb_ref, pgf_ref, sp_ref, agc_ref, low_ref) = rest[4:]

    row0 = (lax.axis_index("grp_0") * 2 + lax.axis_index("grp_1")) * R
    col0 = (lax.axis_index("dev_0") * lax.axis_size("dev_1") + lax.axis_index("dev_1")) * C
    rows_all = lax.axis_size("grp_0") * lax.axis_size("grp_1") * R
    cols_all = lax.axis_size("dev_0") * lax.axis_size("dev_1") * C

    h_ref[...] = jnp.zeros_like(h_ref)
    h_ref[8 : 8 + R, 0:C] = off_ref[...]
    h_ref[0:8, :] = row_offsets(above_ref)
    h_ref[8 + R : OR, :] = row_offsets(below_ref)

    def col_offsets(ref):
        parts = ref[COL_OFF:COL_END, 0:128].astype(F32)
        whole = parts + rolled(parts, -HC, 1) + rolled(parts, -2 * HC, 1)
        return jnp.where(lax.broadcasted_iota(jnp.int32, (OR, 128), 1) < HC, whole, 0.0)

    h_ref[...] = (
        col_offsets(left_ref) + rolled(h_ref[...], HC, 1) + rolled(col_offsets(right_ref), HC + C, 1)
    )
    h = h_ref[...]
    q = lax.broadcasted_iota(jnp.int32, (OR, 128), 0)
    c = lax.broadcasted_iota(jnp.int32, (OR, 128), 1)
    row_id = row0 - 8 + q
    col_id = col0 - HC + c
    inside = (
        (row_id >= 0) & (row_id < rows_all) & (col_id >= 0) & (col_id < cols_all) & (c < EC)
    ).astype(F32)
    s = inverse_roots(h, inside)

    pick_r = lax.broadcasted_iota(jnp.int32, (OR // 2, OR), 1) // 2
    pick_r = jnp.where(pick_r == lax.broadcasted_iota(jnp.int32, (OR // 2, OR), 0), 0.5, 0.0)
    pick_c = lax.broadcasted_iota(jnp.int32, (128, 128), 0) // 2
    pick_c = jnp.where(pick_c == lax.broadcasted_iota(jnp.int32, (128, 128), 1), 0.5, 0.0)
    ph = jnp.dot(pick_r, h, precision=lax.Precision.HIGHEST, preferred_element_type=F32)
    ph = jnp.dot(ph, pick_c, precision=lax.Precision.HIGHEST, preferred_element_type=F32)
    pq = lax.broadcasted_iota(jnp.int32, (OR // 2, 128), 0)
    pc = lax.broadcasted_iota(jnp.int32, (OR // 2, 128), 1)
    prow = row0 // 2 - 4 + pq
    pcol = col0 // 2 - 4 + pc
    pinside = (
        (prow >= 0) & (prow < rows_all // 2) & (pcol >= 0) & (pcol < cols_all // 2) & (pc < QC)
    ).astype(F32)
    ps = inverse_roots(ph, pinside)

    hw_ref[0:OR, :] = fine_windows(h)
    sw_ref[0:OR, :] = fine_windows(s)
    hw_ref[OR : OR + OR // 2, :] = pooled_windows(ph)
    sw_ref[OR : OR + OR // 2, :] = pooled_windows(ps)
    ht, st = transposed(h), transposed(s)
    pht, pst = transposed(ph), transposed(ps)
    k = lax.broadcasted_iota(jnp.int32, (EC, 256), 1)
    i = lax.broadcasted_iota(jnp.int32, (EC, 256), 0)
    block = (k >= EC).astype(jnp.int32) + (k >= 2 * EC).astype(jnp.int32)
    link = -couplings(block - 1, k - block * EC - i)
    for r in range(1, ER - 1):
        at = r + 2
        gap = ht[0:EC, at : at + 1] - hw_ref[at : at + 1, :]
        scale = st[0:EC, at : at + 1] * sw_ref[at : at + 1, :]
        table_ref[2 * (r - 1) * EC : 2 * r * EC, :] = in_two(link * jnp.exp(-gap * gap) * scale)
    k = lax.broadcasted_iota(jnp.int32, (QC, 256), 1)
    i = lax.broadcasted_iota(jnp.int32, (QC, 256), 0)
    block = sum((k >= QC * j).astype(jnp.int32) for j in range(1, 6))
    plinks = [-couplings(block - 1 - j, k - block * QC - i) for j in range(4)]
    for b in range(3):
        at = 2 + 4 * b
        for j in (0, 2):
            both = []
            for jj in (j, j + 1):
                col = at + jj
                gap = pht[0:QC, col : col + 1] - hw_ref[OR + at : OR + at + 1, :]
                scale = pst[0:QC, col : col + 1] * sw_ref[OR + at : OR + at + 1, :]
                both.append(plinks[jj] * jnp.exp(-gap * gap) * scale)
            two = in_two(jnp.concatenate(both, 0))
            at_row = 2 * b * 160 + j * QC
            ptab_ref[at_row : at_row + 2 * QC, :] = two[0 : 2 * QC]
            ptab_ref[at_row + 160 : at_row + 160 + 2 * QC, :] = two[2 * QC :]

    for at, n, ref in ((0, HR, above_ref), (HR, R, px_ref), (HR + R, HR, below_ref)):
        for r in range(0, n, 2):
            side = slice((at + r) * HC, (at + r + 2) * HC)
            left, right = left_ref[side, :].astype(F32), right_ref[side, :].astype(F32)
            middle = ref[r * C : (r + 2) * C, :].astype(F32)
            lines = [left[0:8], middle[0:C], right[0:8], left[8:16], middle[C:], right[8:16]]
            row = (at + r) * EC
            pxe_ref[row : row + 2 * EC, :] = jnp.concatenate(lines, 0).astype(BF)

    left = left_ref[COL_CT:COL_OFF, :].astype(F32)
    right = right_ref[COL_CT:COL_OFF, :].astype(F32)
    for at, n, base, ref in ((0, 3, ROW_CT, above_ref), (3, PR, 0, ct_ref), (3 + PR, 3, ROW_CT, below_ref)):
        for r in range(n):
            e = at + r
            ctf_ref[e * QC : e * QC + 4, :] = left[e * 4 : e * 4 + 4]
            ctf_ref[e * QC + 4 : e * QC + 4 + PC, :] = ref[base + r * PC : base + (r + 1) * PC, :].astype(F32)
            ctf_ref[e * QC + 4 + PC : (e + 1) * QC, :] = right[e * 4 : e * 4 + 4]
    ctb_ref[...] = ctf_ref[...].astype(BF)

    def table_of(r):
        return table_ref[2 * (r - 1) * EC : 2 * r * EC, 0 : 3 * EC]

    for r in range(1, ER - 1):
        one = applied(table_of(r), pxe_ref[(r - 1) * EC : (r + 2) * EC, :])
        f1_ref[(r - 1) * EC : r * EC, :] = one.astype(BF)
        if HR <= r < HR + R:
            f1c_ref[(r - HR) * C : (r - HR + 1) * C, :] = one[HC : HC + C].astype(BF)
    for r in range(2, ER - 2):
        two = 2.0 * applied(table_of(r), f1_ref[(r - 2) * EC : (r + 1) * EC, :])
        two = two - pxe_ref[r * EC : (r + 1) * EC, :].astype(F32)
        f2_ref[(r - 2) * EC : (r - 1) * EC, :] = two.astype(BF)
        if HR <= r < HR + R:
            f2c_ref[(r - HR) * C : (r - HR + 1) * C, :] = two[HC : HC + C].astype(BF)
    poolf_ref[...] = jnp.zeros_like(poolf_ref)
    p1f_ref[...] = jnp.zeros_like(p1f_ref)
    midf_ref[...] = jnp.zeros_like(midf_ref)
    for b in range(6):
        r = 2 + 4 * b
        act = mm(pxe_ref[r * EC : (r + 4) * EC, :], w1_ref[0])
        act = act + mm(f1_ref[(r - 1) * EC : (r + 3) * EC, :], w1_ref[1])
        act = act + mm(f2_ref[(r - 2) * EC : (r + 2) * EC, :], w1_ref[2])
        sig = 1.0 / (1.0 + jnp.exp(-act))
        slope_ref[(r - 2) * EC : (r + 2) * EC, :] = sig * (1.0 + act * (1.0 - sig))
        hid = act * sig
        for n in (0, 1):
            half = hid[:, n * 128 : (n + 1) * 128]
            ref = hid_ref.at[2 * b + n]
            ref[0:EC, :] = half[0:EC] + half[EC : 2 * EC]
            ref[EC : 2 * EC, :] = half[2 * EC : 3 * EC] + half[3 * EC : 4 * EC]
            pooled = 0.25 * (ref[pl.ds(0, EC, stride=2), :] + ref[pl.ds(1, EC, stride=2), :])
            pooled = pooled.astype(BF).astype(F32)
            poolf_ref[(1 + 2 * b) * QC : (3 + 2 * b) * QC, n * 128 : (n + 1) * 128] = pooled
    pb_ref[...] = poolf_ref[...].astype(BF)

    def ptable_of(b):
        return ptab_ref[b * 320 : (b + 1) * 320, 0 : 6 * QC]

    for b in range(3):
        one = applied(ptable_of(b), pb_ref[b * 160 : b * 160 + 6 * QC, :])
        p1f_ref[(1 + 4 * b) * QC : (5 + 4 * b) * QC, :] = one
    p1b_ref[...] = p1f_ref[...].astype(BF)
    for b in range(3):
        two = 2.0 * applied(ptable_of(b), p1b_ref[b * 160 : b * 160 + 6 * QC, :])
        lines = slice((1 + 4 * b) * QC, (5 + 4 * b) * QC)
        p2f_ref[lines, :] = two - poolf_ref[lines, :]
    own = slice(3 * QC, 11 * QC)
    terms = [poolf_ref[own, :].astype(BF), p1f_ref[own, :].astype(BF), p2f_ref[own, :].astype(BF)]
    low_ref[...] = sum(mm(term, w2_ref[n]) for n, term in enumerate(terms))
    for r in range(PR):
        level_ref[r * PC : (r + 1) * PC, :] = low_ref[r * QC + 4 : r * QC + 4 + PC, :].astype(BF)
    col = lax.broadcasted_iota(jnp.int32, (QC, F), 0)
    keep = ((col >= 4) & (col < 4 + PC)).astype(F32)
    cot_own = (ctf_ref[own, :].reshape(PR, QC, F) * keep[None]).reshape(PR * QC, F).astype(BF)
    for n, term in enumerate(terms):
        sums_ref[(3 + n) * F : (4 + n) * F, :] = mm_tn(term, cot_own).astype(sums_ref.dtype)

    cot = ctb_ref[...]
    topb_ref[...] = mm_nt(cot, w2_ref[2]).astype(BF)
    from_one = mm_nt(cot, w2_ref[1])
    for b in range(3):
        lines = slice((1 + 4 * b) * QC, (5 + 4 * b) * QC)
        mid = 2.0 * applied(ptable_of(b), topb_ref[b * 160 : b * 160 + 6 * QC, :])
        midf_ref[lines, :] = from_one[lines] + mid
    midb_ref[...] = midf_ref[...].astype(BF)
    from_zero = mm_nt(cot, w2_ref[0]) - topb_ref[...].astype(F32)
    for b in range(3):
        lines = slice((1 + 4 * b) * QC, (5 + 4 * b) * QC)
        pgf_ref[lines, :] = from_zero[lines] + applied(ptable_of(b), midb_ref[b * 160 : b * 160 + 6 * QC, :])
    for b in range(5):
        u = 2 + 2 * b
        grad = 0.25 * pgf_ref[u * QC : (u + 2) * QC, :]
        for n in (0, 1):
            ref = sp_ref.at[2 * b + n]
            ref[pl.ds(0, 2 * QC, stride=2), :] = grad[:, n * 128 : (n + 1) * 128]
            ref[pl.ds(1, 2 * QC, stride=2), :] = grad[:, n * 128 : (n + 1) * 128]
        for n in range(4):
            r = 2 * u + n
            lines = slice((n // 2) * EC, (n // 2 + 1) * EC)
            spread = jnp.concatenate([sp_ref[2 * b, lines, :], sp_ref[2 * b + 1, lines, :]], 1)
            grad_row = spread * slope_ref[(r - 2) * EC : (r - 1) * EC, :]
            grad_ref[(r - 4) * EC : (r - 3) * EC, :] = grad_row.astype(BF)
            if HR <= r < HR + R:
                agc_ref[(r - HR) * C : (r - HR + 1) * C, :] = grad_row[HC : HC + C].astype(BF)
    for n, ref in enumerate((px_ref, f1c_ref, f2c_ref)):
        sums_ref[n * F : (n + 1) * F, :] = mm_tn(ref[...], agc_ref[...]).astype(sums_ref.dtype)


def main_stage(pixels, cotangent, offsets, first_weights, second_weights, got):
    fine, pooled = ER * EC, QR * QC
    scratch = [
        ((OR, 128), F32),
        ((OR + OR // 2, 256), F32),
        ((OR + OR // 2, 256), F32),
        ((fine, F), BF),
        ((26 * EC, F), BF),
        ((24 * EC, F), BF),
        ((R * C, F), BF),
        ((R * C, F), BF),
        ((24 * EC, F), F32),
        ((12, 2 * EC, 128), F32),
        ((pooled, F), F32),
        ((pooled, F), F32),
        ((pooled, F), F32),
        ((pooled, F), F32),
        ((960, 256), BF),
        ((pooled, F), BF),
        ((pooled, F), BF),
        ((pooled, F), BF),
        ((pooled, F), BF),
        ((pooled, F), F32),
        ((pooled, F), BF),
        ((pooled, F), F32),
        ((10, 2 * EC, 128), F32),
        ((R * C, F), BF),
        ((PR * QC, F), F32),
    ]
    return pl.pallas_call(
        main_kernel,
        out_shape=[
            jax.ShapeDtypeStruct((PR * PC, F), BF),
            jax.ShapeDtypeStruct((6 * F, F), BF),
            jax.ShapeDtypeStruct((52 * EC, 256), BF),
            jax.ShapeDtypeStruct((20 * EC, F), BF),
        ],
        scratch_shapes=[pltpu.VMEM(shape, dtype) for shape, dtype in scratch],
        compiler_params=pltpu.CompilerParams(vmem_limit_bytes=56 << 20),
        name="main",
    )(pixels, cotangent, offsets, first_weights, second_weights, *got)


def tail_kernel(table_ref, grad_ref, w_ref, out_ref, top_ref, mid_ref):
    top_ref[...] = mm_nt(grad_ref[...], w_ref[2]).astype(BF)
    for b in range(9):
        r = 5 + 2 * b
        base = mm_nt(grad_ref[(r - 4) * EC : (r - 2) * EC, :], w_ref[1])
        for n in (0, 1):
            table = table_ref[2 * (r + n - 1) * EC : 2 * (r + n) * EC, 0 : 3 * EC]
            mid = 2.0 * applied(table, top_ref[(r + n - 5) * EC : (r + n - 2) * EC, :])
            mid = base[n * EC : (n + 1) * EC] + mid
            mid_ref[(r + n - 5) * EC : (r + n - 4) * EC, :] = mid.astype(BF)
    for b in range(8):
        r = 6 + 2 * b
        base = mm_nt(grad_ref[(r - 4) * EC : (r - 2) * EC, :], w_ref[0])
        base = base - top_ref[(r - 4) * EC : (r - 2) * EC, :].astype(F32)
        for n in (0, 1):
            table = table_ref[2 * (r + n - 1) * EC : 2 * (r + n) * EC, 0 : 3 * EC]
            line = base[n * EC : (n + 1) * EC] + applied(table, mid_ref[(r + n - 6) * EC : (r + n - 3) * EC, :])
            at = (r + n - HR) * C
            out_ref[at : at + C, :] = line[HC : HC + C].astype(BF)


def tail_stage(table, grad, first_weights):
    return pl.pallas_call(
        tail_kernel,
        out_shape=jax.ShapeDtypeStruct((R * C, F), BF),
        scratch_shapes=[pltpu.VMEM((20 * EC, F), BF), pltpu.VMEM((18 * EC, F), BF)],
        compiler_params=pltpu.CompilerParams(vmem_limit_bytes=56 << 20),
        name="tail",
    )(table, grad, first_weights)


def sum_at_owner(value, axes):
    tiles = lax.all_to_all(value.reshape(lax.axis_size(axes), -1, F), axes, 0, 0, tiled=True)
    return jnp.sum(tiles.astype(F32), axis=0).astype(BF)


def sent_to_all(value, axes):
    copies = jnp.broadcast_to(value, (lax.axis_size(axes), *value.shape))
    return lax.all_to_all(copies, axes, 0, 0, tiled=True)


def total_of(value):
    value = sum_at_owner(sum_at_owner(value, ("grp_1",)), DEV)
    value = jnp.sum(sent_to_all(value, ("grp_0",)).astype(F32), axis=0).astype(BF)
    value = sent_to_all(value, DEV).reshape(-1, F)
    return sent_to_all(value, ("grp_1",)).reshape(-1, F)


def clip_kernel(sums_ref, first_ref, second_ref):
    total = jnp.zeros((8, F), F32)
    for n in range(6):
        part = sums_ref[n * F : (n + 1) * F, :].astype(F32)
        total = total + jnp.sum((part * part).reshape(F // 8, 8, F), axis=0)
    square_sum = jnp.sum(jnp.sum(total, axis=1, keepdims=True), axis=0, keepdims=True)
    factor = jnp.minimum(1.0, 2.0 * F * lax.rsqrt(square_sum + 1e-06))
    for n in range(3):
        first_ref[n] = sums_ref[n * F : (n + 1) * F, :].astype(F32) * factor
        second_ref[n] = sums_ref[(3 + n) * F : (4 + n) * F, :].astype(F32) * factor


def clipped(sums):
    shape = jax.ShapeDtypeStruct((3, F, F), F32)
    return pl.pallas_call(clip_kernel, out_shape=[shape, shape], name="clip")(sums)


def shards(pixels, offsets, first_weights, second_weights, cotangent):
    px = pixels.reshape(R * C, F)
    ct = cotangent.reshape(PR * PC, F)
    above, below = exchanged(*row_messages(px, ct, offsets), GRP)
    left, right = exchanged(*col_messages(px, ct, offsets, above, below), DEV)
    got = (above, below, left, right)
    level, sums, table, grad = main_stage(px, ct, offsets, first_weights, second_weights, got)
    first, second = clipped(total_of(sums))
    grad_pixels = tail_stage(table, grad, first_weights)
    return grad_pixels.reshape(R, C, F), first, second, level.reshape(PR, PC, F)


def solution(mesh):
    finer = Mesh(mesh.devices.reshape(-1, 2, 4, mesh.devices.shape[1] // 4), EVERY)
    in_specs = (P(GRP, DEV, None), P(GRP, DEV), P(), P(), P(GRP, DEV, None))
    out_specs = (P(GRP, DEV, None), P(), P(), P(GRP, DEV, None))
    return jax.shard_map(
        shards, mesh=finer, in_specs=in_specs, out_specs=out_specs, check_vma=False
    )
```

```python
import functools

import jax
import jax.numpy as jnp
from jax import lax
from jax.experimental import pallas as pl
from jax.experimental.pallas import tpu as pltpu
from jax.sharding import Mesh
from jax.sharding import PartitionSpec as P

GRP = ("grp_0", "grp_1")
DEV = ("dev_0", "dev_1")
EVERY = GRP + DEV
BF = jnp.bfloat16
F32 = jnp.float32

R, C, F = 16, 64, 256
PR, PC = R // 2, C // 2
HR, HC = 6, 8
ER, EC = R + 2 * HR, C + 2 * HC
QR, QC = PR + 6, PC + 8
OR = R + 16

STEPS = (
    (-1, 0, 1.0),
    (1, 0, 1.0),
    (0, -1, 1.0),
    (0, 1, 1.0),
    (-1, -1, 0.5),
    (-1, 1, 0.5),
    (1, -1, 0.5),
    (1, 1, 0.5),
)


def mm(a, b):
    return lax.dot_general(a, b, (((1,), (0,)), ((), ())), preferred_element_type=F32)


def mm_nt(a, b):
    return lax.dot_general(a, b, (((1,), (1,)), ((), ())), preferred_element_type=F32)


def mm_tn(a, b):
    return lax.dot_general(a, b, (((0,), (0,)), ((), ())), preferred_element_type=F32)


ROW_CT = HR * C
ROW_OFF = ROW_CT + 3 * PC
ROW_END = ROW_OFF + 32
COL_CT = ER * HC
COL_OFF = COL_CT + 64
COL_END = COL_OFF + OR


def on_chip(*arrays):
    return [pltpu.with_memory_space_constraint(a, pltpu.VMEM) for a in arrays]


def in_hbm(*arrays):
    return [pltpu.with_memory_space_constraint(a, pltpu.HBM) for a in arrays]


def rolled(x, shift, axis):
    return pltpu.roll(x, shift % x.shape[axis], axis)


def in_parts(x):
    high = x.astype(BF).astype(F32)
    left = x - high
    middle = left.astype(BF).astype(F32)
    return high, middle, left - middle


def started(sems, pairs):
    copies = [pltpu.make_async_copy(src, dst, sems.at[n]) for n, (src, dst) in enumerate(pairs)]
    for copy in copies:
        copy.start()
    return copies


def row_pack_kernel(px_ref, ct_ref, px_rows, ct_rows, off_ref, *rest):
    up_ref, down_ref, pxl_ref, pxr_ref, ctl_ref, ctr_ref, wide, off_buf, sems = rest
    pairs = [(off_ref, off_buf)]
    for out, px_at, ct_at in ((up_ref, 0, 0), (down_ref, R - HR, PR - 3)):
        for ref, at, size, to in ((px_ref, px_at * C, HR * C, 0), (ct_ref, ct_at * PC, 3 * PC, ROW_CT)):
            pairs.append((ref.at[pl.ds(at, size), :], out.at[pl.ds(to, size), :]))
    pairs += [
        (px_rows.at[:, pl.ds(0, 16), :], pxl_ref),
        (px_rows.at[:, pl.ds(C - 16, 16), :], pxr_ref),
        (ct_rows.at[:, pl.ds(0, 16), :], ctl_ref),
        (ct_rows.at[:, pl.ds(PC - 16, 16), :], ctr_ref),
    ]
    copies = started(sems, pairs)
    wide[...] = jnp.zeros_like(wide)
    copies[0].wait()
    wide[:, 0:C] = off_buf[...]
    for out, off_at in ((up_ref, 0), (down_ref, R - 8)):
        high, middle, low = in_parts(wide[off_at : off_at + 8, :])
        packed = jnp.concatenate([high, middle, low, jnp.zeros_like(low)], 0)
        out[ROW_OFF:ROW_END, :] = jnp.concatenate([packed, jnp.zeros_like(packed)], 1).astype(BF)
    for copy in copies[1:]:
        copy.wait()


def row_messages(pixels, cotangent, offsets):
    return pl.pallas_call(
        row_pack_kernel,
        in_specs=[pl.BlockSpec(memory_space=pltpu.HBM)] * 5,
        out_shape=[
            pltpu.VMEM((ROW_END, F), BF),
            pltpu.VMEM((ROW_END, F), BF),
            pltpu.VMEM((R, 16, F), BF),
            pltpu.VMEM((R, 16, F), BF),
            pltpu.VMEM((PR, 16, F), BF),
            pltpu.VMEM((PR, 16, F), BF),
            pltpu.VMEM((R, 128), F32),
        ],
        scratch_shapes=[pltpu.VMEM((R, C), F32), pltpu.SemaphoreType.DMA((9,))],
        compiler_params=pltpu.CompilerParams(vmem_limit_bytes=4 << 20),
        name="row_pack",
    )(*in_hbm(pixels, cotangent, pixels.reshape(R, C, F), cotangent.reshape(PR, PC, F), offsets))


def row_offsets(ref):
    parts = ref[ROW_OFF:ROW_END, 0:128].astype(F32)
    return parts[0:8] + parts[8:16] + parts[16:24]


def col_pack_kernel(*refs):
    pxl_ref, pxr_ref, ctl_ref, ctr_ref, off_ref, above_ref, below_ref, left_ref, right_ref, wide = refs
    wide[8 : 8 + R, :] = off_ref[...]
    wide[0:8, :] = row_offsets(above_ref)
    wide[8 + R : OR, :] = row_offsets(below_ref)
    lane = lax.broadcasted_iota(jnp.int32, (OR, 128), 1)
    near = lax.broadcasted_iota(jnp.int32, (8, F), 0) < 4
    for out, px_ref, ct_ref, px_at, ct_at, half in (
        (left_ref, pxl_ref, ctl_ref, 0, 0, slice(0, 8)),
        (right_ref, pxr_ref, ctr_ref, C - 16, PC - 16, slice(8, 16)),
    ):

        def line(ref, k, base, width, at):
            if ref is above_ref or ref is below_ref:
                return ref[base + k * width + at : base + k * width + at + 16, :].astype(F32)[half]
            return ref[k].astype(F32)[half]

        for first, n, ref in ((0, HR, above_ref), (HR, R, px_ref), (HR + R, HR, below_ref)):
            for r in range(0, n, 2):
                tiles = [line(ref, k, 0, C, px_at) for k in (r, r + 1)]
                at = (first + r) * HC
                out[at : at + 16, :] = jnp.concatenate(tiles, 0).astype(BF)
        lines = []
        for n, ref in ((3, above_ref), (PR, ct_ref), (3, below_ref)):
            lines += [line(ref, k, ROW_CT, PC, ct_at) for k in range(n)]
        tiles = []
        for e in range(0, QR, 2):
            first, second = lines[e], lines[e + 1]
            if out is left_ref:
                second = rolled(second, 4, 0)
            else:
                first = rolled(first, 4, 0)
            tiles.append(jnp.where(near, first, second))
        tiles.append(jnp.zeros((8, F), F32))
        out[COL_CT:COL_OFF, :] = jnp.concatenate(tiles, 0).astype(BF)
        part = wide[...] if out is left_ref else rolled(wide[...], HC - C, 1)
        high, middle, low = in_parts(jnp.where(lane < HC, part, 0.0))
        packed = high + rolled(middle, HC, 1) + rolled(low, 2 * HC, 1)
        out[COL_OFF:COL_END, :] = jnp.concatenate([packed, jnp.zeros_like(packed)], 1).astype(BF)


def col_messages(*parts):
    shape = pltpu.VMEM((COL_END, F), BF)
    return pl.pallas_call(
        col_pack_kernel,
        out_shape=[shape, shape],
        scratch_shapes=[pltpu.VMEM((OR, 128), F32)],
        compiler_params=pltpu.CompilerParams(vmem_limit_bytes=4 << 20),
        name="col_pack",
    )(*on_chip(*parts))


def exchanged(first, last, axis):
    count = lax.axis_size(axis)
    forward = [(i, i + 1) for i in range(count - 1)]
    backward = [(i + 1, i) for i in range(count - 1)]
    return lax.ppermute(last, axis, forward), lax.ppermute(first, axis, backward)


def inverse_roots(h, inside):
    degree = jnp.zeros_like(h)
    for row_step, col_step, coupling in STEPS:
        other = rolled(rolled(h, -row_step, 0), -col_step, 1)
        present = rolled(rolled(inside, -row_step, 0), -col_step, 1)
        degree = degree + coupling * present * jnp.exp(-(h - other) * (h - other))
    return lax.rsqrt(degree + 1.0 - inside) * inside


def couplings(row_gap, col_gap):
    near = jnp.abs(col_gap)
    side = jnp.where(near == 0, 1.0, jnp.where(near == 1, 0.5, 0.0))
    own = jnp.where(near == 1, 1.0, 0.0)
    return jnp.where(row_gap == 0, own, jnp.where(jnp.abs(row_gap) == 1, side, 0.0))


def fine_windows(x):
    lane = lax.broadcasted_iota(jnp.int32, x.shape, 1)
    over = rolled(x, EC, 1)
    low = jnp.where(lane < EC, rolled(x, 1, 0), over)
    high = jnp.where(lane < 2 * EC - 128, over, rolled(rolled(x, -1, 0), 2 * EC - 128, 1))
    return jnp.concatenate([low, high], 1)


def pooled_windows(x):
    lane = lax.broadcasted_iota(jnp.int32, x.shape, 1)
    rows = [rolled(rolled(x, 1 - j, 0), QC * j, 1) for j in range(6)]
    low = jnp.where(
        lane < QC,
        rows[0],
        jnp.where(lane < 2 * QC, rows[1], jnp.where(lane < 3 * QC, rows[2], rows[3])),
    )
    high = jnp.where(
        lane < 4 * QC - 128,
        rows[3],
        jnp.where(
            lane < 5 * QC - 128, rows[4], jnp.where(lane < 6 * QC - 128, rows[5], 0.0)
        ),
    )
    return jnp.concatenate([low, high], 1)


def in_two(x):
    high = x.astype(BF)
    return jnp.concatenate([high, (x - high.astype(F32)).astype(BF)], 0)


def applied(table, values):
    both = mm(table, values)
    half = both.shape[0] // 2
    return both[0:half] + both[half:]


def transposed(x):
    if x.shape[0] < 128:
        x = jnp.concatenate([x, jnp.zeros((128 - x.shape[0], 128), F32)], 0)
    return x.T


def main_kernel(px_hbm, ct_hbm, w1_hbm, w2_hbm, off_ref, above_ref, below_ref, left_ref, right_ref, *rest):
    terms_hbm, keep_ref, send_ref, table_ref, grad_hbm = rest[:5]
    (h_ref, hw_ref, sw_ref, pxe_ref, f1_ref, f2_ref, f1c_ref, f2c_ref, slope_ref, hid_ref,
     poolf_ref, p1f_ref, p2f_ref, ctf_ref, ptab_ref, pb_ref, p1b_ref, ctb_ref, topb_ref,
     midf_ref, midb_ref, pgf_ref, sp_ref, agc_ref, halves_ref, px_ref, ct_ref, w1_ref, w2_ref,
     terms_ref, grad_ref, sems, out_sems) = rest[5:]
    copies = started(
        sems, [(px_hbm, px_ref), (ct_hbm, ct_ref), (w1_hbm, w1_ref), (w2_hbm, w2_ref)]
    )
    core = lax.axis_index("grp_1")

    row0 = (lax.axis_index("grp_0") * 2 + lax.axis_index("grp_1")) * R
    col0 = (lax.axis_index("dev_0") * lax.axis_size("dev_1") + lax.axis_index("dev_1")) * C
    rows_all = lax.axis_size("grp_0") * lax.axis_size("grp_1") * R
    cols_all = lax.axis_size("dev_0") * lax.axis_size("dev_1") * C

    h_ref[8 : 8 + R, :] = off_ref[...]
    h_ref[0:8, :] = row_offsets(above_ref)
    h_ref[8 + R : OR, :] = row_offsets(below_ref)

    def col_offsets(ref):
        parts = ref[COL_OFF:COL_END, 0:128].astype(F32)
        whole = parts + rolled(parts, -HC, 1) + rolled(parts, -2 * HC, 1)
        return jnp.where(lax.broadcasted_iota(jnp.int32, (OR, 128), 1) < HC, whole, 0.0)

    h_ref[...] = (
        col_offsets(left_ref) + rolled(h_ref[...], HC, 1) + rolled(col_offsets(right_ref), HC + C, 1)
    )
    h = h_ref[...]
    q = lax.broadcasted_iota(jnp.int32, (OR, 128), 0)
    c = lax.broadcasted_iota(jnp.int32, (OR, 128), 1)
    row_id = row0 - 8 + q
    col_id = col0 - HC + c
    inside = (
        (row_id >= 0) & (row_id < rows_all) & (col_id >= 0) & (col_id < cols_all) & (c < EC)
    ).astype(F32)
    s = inverse_roots(h, inside)

    pick_r = lax.broadcasted_iota(jnp.int32, (OR // 2, OR), 1) // 2
    pick_r = jnp.where(pick_r == lax.broadcasted_iota(jnp.int32, (OR // 2, OR), 0), 0.5, 0.0)
    pick_c = lax.broadcasted_iota(jnp.int32, (128, 128), 0) // 2
    pick_c = jnp.where(pick_c == lax.broadcasted_iota(jnp.int32, (128, 128), 1), 0.5, 0.0)
    ph = jnp.dot(pick_r, h, precision=lax.Precision.HIGHEST, preferred_element_type=F32)
    ph = jnp.dot(ph, pick_c, precision=lax.Precision.HIGHEST, preferred_element_type=F32)
    pq = lax.broadcasted_iota(jnp.int32, (OR // 2, 128), 0)
    pc = lax.broadcasted_iota(jnp.int32, (OR // 2, 128), 1)
    prow = row0 // 2 - 4 + pq
    pcol = col0 // 2 - 4 + pc
    pinside = (
        (prow >= 0) & (prow < rows_all // 2) & (pcol >= 0) & (pcol < cols_all // 2) & (pc < QC)
    ).astype(F32)
    ps = inverse_roots(ph, pinside)

    hw_ref[0:OR, :] = fine_windows(h)
    sw_ref[0:OR, :] = fine_windows(s)
    hw_ref[OR : OR + OR // 2, :] = pooled_windows(ph)
    sw_ref[OR : OR + OR // 2, :] = pooled_windows(ps)
    ht, st = transposed(h), transposed(s)
    pht, pst = transposed(ph), transposed(ps)
    k = lax.broadcasted_iota(jnp.int32, (EC, 256), 1)
    i = lax.broadcasted_iota(jnp.int32, (EC, 256), 0)
    block = (k >= EC).astype(jnp.int32) + (k >= 2 * EC).astype(jnp.int32)
    link = -couplings(block - 1, k - block * EC - i)
    for r in range(1, ER - 1):
        at = r + 2
        gap = ht[0:EC, at : at + 1] - hw_ref[at : at + 1, :]
        scale = st[0:EC, at : at + 1] * sw_ref[at : at + 1, :]
        table_ref[2 * (r - 1) * EC : 2 * r * EC, :] = in_two(link * jnp.exp(-gap * gap) * scale)
    k = lax.broadcasted_iota(jnp.int32, (QC, 256), 1)
    i = lax.broadcasted_iota(jnp.int32, (QC, 256), 0)
    block = sum((k >= QC * j).astype(jnp.int32) for j in range(1, 6))
    plinks = [-couplings(block - 1 - j, k - block * QC - i) for j in range(4)]
    for b in range(3):
        at = 2 + 4 * b
        for j in (0, 2):
            both = []
            for jj in (j, j + 1):
                col = at + jj
                gap = pht[0:QC, col : col + 1] - hw_ref[OR + at : OR + at + 1, :]
                scale = pst[0:QC, col : col + 1] * sw_ref[OR + at : OR + at + 1, :]
                both.append(plinks[jj] * jnp.exp(-gap * gap) * scale)
            two = in_two(jnp.concatenate(both, 0))
            at_row = 2 * b * 160 + j * QC
            ptab_ref[at_row : at_row + 2 * QC, :] = two[0 : 2 * QC]
            ptab_ref[at_row + 160 : at_row + 160 + 2 * QC, :] = two[2 * QC :]

    copies[0].wait()
    copies[1].wait()
    for at, n, ref in ((0, HR, above_ref), (HR, R, px_ref), (HR + R, HR, below_ref)):
        for r in range(0, n, 2):
            side = slice((at + r) * HC, (at + r + 2) * HC)
            left, right = left_ref[side, :].astype(F32), right_ref[side, :].astype(F32)
            middle = ref[r * C : (r + 2) * C, :].astype(F32)
            lines = [left[0:8], middle[0:C], right[0:8], left[8:16], middle[C:], right[8:16]]
            row = (at + r) * EC
            pxe_ref[row : row + 2 * EC, :] = jnp.concatenate(lines, 0).astype(BF)

    left = left_ref[COL_CT:COL_OFF, :].astype(F32)
    right = right_ref[COL_CT:COL_OFF, :].astype(F32)
    for at, n, base, ref in ((0, 3, ROW_CT, above_ref), (3, PR, 0, ct_ref), (3 + PR, 3, ROW_CT, below_ref)):
        for r in range(n):
            e = at + r
            ctf_ref[e * QC : e * QC + 4, :] = left[e * 4 : e * 4 + 4]
            ctf_ref[e * QC + 4 : e * QC + 4 + PC, :] = ref[base + r * PC : base + (r + 1) * PC, :].astype(F32)
            ctf_ref[e * QC + 4 + PC : (e + 1) * QC, :] = right[e * 4 : e * 4 + 4]
    ctb_ref[...] = ctf_ref[...].astype(BF)

    copies[2].wait()
    copies[3].wait()

    def table_of(r):
        return table_ref[2 * (r - 1) * EC : 2 * r * EC, 0 : 3 * EC]

    for r in range(1, ER - 1):
        one = applied(table_of(r), pxe_ref[(r - 1) * EC : (r + 2) * EC, :])
        f1_ref[(r - 1) * EC : r * EC, :] = one.astype(BF)
        if HR <= r < HR + R:
            f1c_ref[(r - HR) * C : (r - HR + 1) * C, :] = one[HC : HC + C].astype(BF)
    for r in range(2, ER - 2):
        two = 2.0 * applied(table_of(r), f1_ref[(r - 2) * EC : (r + 1) * EC, :])
        two = two - pxe_ref[r * EC : (r + 1) * EC, :].astype(F32)
        f2_ref[(r - 2) * EC : (r - 1) * EC, :] = two.astype(BF)
        if HR <= r < HR + R:
            f2c_ref[(r - HR) * C : (r - HR + 1) * C, :] = two[HC : HC + C].astype(BF)
    poolf_ref[...] = jnp.zeros_like(poolf_ref)
    p1f_ref[...] = jnp.zeros_like(p1f_ref)
    midf_ref[...] = jnp.zeros_like(midf_ref)
    for b in range(6):
        r = 2 + 4 * b
        act = mm(pxe_ref[r * EC : (r + 4) * EC, :], w1_ref[0])
        act = act + mm(f1_ref[(r - 1) * EC : (r + 3) * EC, :], w1_ref[1])
        act = act + mm(f2_ref[(r - 2) * EC : (r + 2) * EC, :], w1_ref[2])
        sig = 1.0 / (1.0 + jnp.exp(-act))
        slope_ref[(r - 2) * EC : (r + 2) * EC, :] = sig * (1.0 + act * (1.0 - sig))
        hid = act * sig
        for n in (0, 1):
            half = hid[:, n * 128 : (n + 1) * 128]
            ref = hid_ref.at[2 * b + n]
            ref[0:EC, :] = half[0:EC] + half[EC : 2 * EC]
            ref[EC : 2 * EC, :] = half[2 * EC : 3 * EC] + half[3 * EC : 4 * EC]
            pooled = 0.25 * (ref[pl.ds(0, EC, stride=2), :] + ref[pl.ds(1, EC, stride=2), :])
            pooled = pooled.astype(BF).astype(F32)
            poolf_ref[(1 + 2 * b) * QC : (3 + 2 * b) * QC, n * 128 : (n + 1) * 128] = pooled
    pb_ref[...] = poolf_ref[...].astype(BF)

    def ptable_of(b):
        return ptab_ref[b * 320 : (b + 1) * 320, 0 : 6 * QC]

    for b in range(3):
        one = applied(ptable_of(b), pb_ref[b * 160 : b * 160 + 6 * QC, :])
        p1f_ref[(1 + 4 * b) * QC : (5 + 4 * b) * QC, :] = one
    p1b_ref[...] = p1f_ref[...].astype(BF)
    for b in range(3):
        two = 2.0 * applied(ptable_of(b), p1b_ref[b * 160 : b * 160 + 6 * QC, :])
        lines = slice((1 + 4 * b) * QC, (5 + 4 * b) * QC)
        p2f_ref[lines, :] = two - poolf_ref[lines, :]
    own = slice(3 * QC, 11 * QC)
    terms = [poolf_ref[own, :].astype(BF), p1f_ref[own, :].astype(BF), p2f_ref[own, :].astype(BF)]
    for n, term in enumerate(terms):
        terms_ref[n] = term
    outward = [pltpu.make_async_copy(terms_ref, terms_hbm, out_sems.at[0])]
    outward[0].start()
    col = lax.broadcasted_iota(jnp.int32, (QC, F), 0)
    keep = ((col >= 4) & (col < 4 + PC)).astype(F32)
    cot_own = (ctf_ref[own, :].reshape(PR, QC, F) * keep[None]).reshape(PR * QC, F).astype(BF)
    for n, term in enumerate(terms):
        halves_ref[1 - core, n * F : (n + 1) * F, :] = mm_tn(term, cot_own).astype(BF)

    cot = ctb_ref[...]
    topb_ref[...] = mm_nt(cot, w2_ref[2]).astype(BF)
    from_one = mm_nt(cot, w2_ref[1])
    for b in range(3):
        lines = slice((1 + 4 * b) * QC, (5 + 4 * b) * QC)
        mid = 2.0 * applied(ptable_of(b), topb_ref[b * 160 : b * 160 + 6 * QC, :])
        midf_ref[lines, :] = from_one[lines] + mid
    midb_ref[...] = midf_ref[...].astype(BF)
    from_zero = mm_nt(cot, w2_ref[0]) - topb_ref[...].astype(F32)
    for b in range(3):
        lines = slice((1 + 4 * b) * QC, (5 + 4 * b) * QC)
        pgf_ref[lines, :] = from_zero[lines] + applied(ptable_of(b), midb_ref[b * 160 : b * 160 + 6 * QC, :])
    for b in range(5):
        u = 2 + 2 * b
        grad = 0.25 * pgf_ref[u * QC : (u + 2) * QC, :]
        for n in (0, 1):
            ref = sp_ref.at[2 * b + n]
            ref[pl.ds(0, 2 * QC, stride=2), :] = grad[:, n * 128 : (n + 1) * 128]
            ref[pl.ds(1, 2 * QC, stride=2), :] = grad[:, n * 128 : (n + 1) * 128]
        for n in range(4):
            r = 2 * u + n
            lines = slice((n // 2) * EC, (n // 2 + 1) * EC)
            spread = jnp.concatenate([sp_ref[2 * b, lines, :], sp_ref[2 * b + 1, lines, :]], 1)
            grad_row = spread * slope_ref[(r - 2) * EC : (r - 1) * EC, :]
            grad_ref[(r - 4) * EC : (r - 3) * EC, :] = grad_row.astype(BF)
            if HR <= r < HR + R:
                agc_ref[(r - HR) * C : (r - HR + 1) * C, :] = grad_row[HC : HC + C].astype(BF)
    outward.append(pltpu.make_async_copy(grad_ref, grad_hbm, out_sems.at[1]))
    outward[1].start()
    for n, ref in enumerate((px_ref, f1c_ref, f2c_ref)):
        halves_ref[core, n * F : (n + 1) * F, :] = mm_tn(ref[...], agc_ref[...]).astype(BF)
    keep_ref[...] = halves_ref[0]
    send_ref[...] = halves_ref[1]
    for copy in outward:
        copy.wait()


def main_stage(pixels, cotangent, offsets, first_weights, second_weights, got):
    fine, pooled = ER * EC, QR * QC
    scratch = [
        ((OR, 128), F32),
        ((OR + OR // 2, 256), F32),
        ((OR + OR // 2, 256), F32),
        ((fine, F), BF),
        ((26 * EC, F), BF),
        ((24 * EC, F), BF),
        ((R * C, F), BF),
        ((R * C, F), BF),
        ((24 * EC, F), F32),
        ((12, 2 * EC, 128), F32),
        ((pooled, F), F32),
        ((pooled, F), F32),
        ((pooled, F), F32),
        ((pooled, F), F32),
        ((960, 256), BF),
        ((pooled, F), BF),
        ((pooled, F), BF),
        ((pooled, F), BF),
        ((pooled, F), BF),
        ((pooled, F), F32),
        ((pooled, F), BF),
        ((pooled, F), F32),
        ((10, 2 * EC, 128), F32),
        ((R * C, F), BF),
        ((2, 3 * F, F), BF),
        ((R * C, F), BF),
        ((PR * PC, F), BF),
        ((3, F, F), BF),
        ((3, F, F), BF),
        ((3, PR * QC, F), BF),
        ((20 * EC, F), BF),
    ]
    return pl.pallas_call(
        main_kernel,
        out_shape=[
            pltpu.HBM((3, PR * QC, F), BF),
            pltpu.VMEM((3 * F, F), BF),
            pltpu.VMEM((3 * F, F), BF),
            pltpu.VMEM((52 * EC, 256), BF),
            pltpu.HBM((20 * EC, F), BF),
        ],
        in_specs=[pl.BlockSpec(memory_space=pl.ANY)] * 4
        + [pl.BlockSpec(memory_space=pltpu.VMEM)] * 5,
        scratch_shapes=[pltpu.VMEM(shape, dtype) for shape, dtype in scratch]
        + [pltpu.SemaphoreType.DMA((4,)), pltpu.SemaphoreType.DMA((2,))],
        compiler_params=pltpu.CompilerParams(vmem_limit_bytes=20 << 20),
        name="main",
    )(pixels, cotangent, first_weights, second_weights, *on_chip(offsets, *got))


def tail_kernel(terms_ref, table_ref, grad_ref, w_ref, w2_ref, out_ref, level_ref, top_ref, mid_ref, low_ref):
    top_ref[...] = mm_nt(grad_ref[...], w_ref[2]).astype(BF)
    for b in range(9):
        r = 5 + 2 * b
        base = mm_nt(grad_ref[(r - 4) * EC : (r - 2) * EC, :], w_ref[1])
        for n in (0, 1):
            table = table_ref[2 * (r + n - 1) * EC : 2 * (r + n) * EC, 0 : 3 * EC]
            mid = 2.0 * applied(table, top_ref[(r + n - 5) * EC : (r + n - 2) * EC, :])
            mid = base[n * EC : (n + 1) * EC] + mid
            mid_ref[(r + n - 5) * EC : (r + n - 4) * EC, :] = mid.astype(BF)
    for b in range(8):
        r = 6 + 2 * b
        base = mm_nt(grad_ref[(r - 4) * EC : (r - 2) * EC, :], w_ref[0])
        base = base - top_ref[(r - 4) * EC : (r - 2) * EC, :].astype(F32)
        for n in (0, 1):
            table = table_ref[2 * (r + n - 1) * EC : 2 * (r + n) * EC, 0 : 3 * EC]
            line = base[n * EC : (n + 1) * EC] + applied(table, mid_ref[(r + n - 6) * EC : (r + n - 3) * EC, :])
            at = (r + n - HR) * C
            out_ref[at : at + C, :] = line[HC : HC + C].astype(BF)
    low_ref[...] = sum(mm(terms_ref[n], w2_ref[n]) for n in range(3))
    for r in range(PR):
        level_ref[r * PC : (r + 1) * PC, :] = low_ref[r * QC + 4 : r * QC + 4 + PC, :].astype(BF)


def tail_stage(terms, table, grad, first_weights, second_weights):
    return pl.pallas_call(
        tail_kernel,
        out_shape=[
            jax.ShapeDtypeStruct((R * C, F), BF),
            jax.ShapeDtypeStruct((PR * PC, F), BF),
        ],
        scratch_shapes=[
            pltpu.VMEM((20 * EC, F), BF),
            pltpu.VMEM((18 * EC, F), BF),
            pltpu.VMEM((PR * QC, F), F32),
        ],
        compiler_params=pltpu.CompilerParams(vmem_limit_bytes=8 << 20),
        name="tail",
    )(*in_hbm(terms), *on_chip(table), *in_hbm(grad), first_weights, second_weights)


def sum_at_owner(value, axes):
    tiles = lax.all_to_all(value.reshape(lax.axis_size(axes), -1, F), axes, 0, 0, tiled=True)
    return jnp.sum(tiles.astype(F32), axis=0).astype(BF)


def sent_to_all(value, axes):
    copies = jnp.broadcast_to(value, (lax.axis_size(axes), *value.shape))
    return lax.all_to_all(copies, axes, 0, 0, tiled=True)


def swapped(value):
    return lax.ppermute(value, "grp_1", [(0, 1), (1, 0)])


def total_of(keep, send):
    value = (keep.astype(F32) + swapped(send).astype(F32)).astype(BF)
    value = sum_at_owner(value, DEV)
    value = jnp.sum(sent_to_all(value, ("grp_0",)).astype(F32), axis=0).astype(BF)
    return sent_to_all(value, DEV).reshape(-1, F)


def clip_kernel(own_ref, other_ref, first_ref, second_ref):
    total = jnp.zeros((8, F), F32)
    for ref in (own_ref, other_ref):
        for n in range(3):
            part = ref[n * F : (n + 1) * F, :].astype(F32)
            total = total + jnp.sum((part * part).reshape(F // 8, 8, F), axis=0)
    square_sum = jnp.sum(jnp.sum(total, axis=1, keepdims=True), axis=0, keepdims=True)
    factor = jnp.minimum(1.0, 2.0 * F * lax.rsqrt(square_sum + 1e-06))
    is_first = lax.axis_index("grp_1") == 0
    for n in range(3):
        own = own_ref[n * F : (n + 1) * F, :].astype(F32) * factor
        other = other_ref[n * F : (n + 1) * F, :].astype(F32) * factor
        first_ref[n] = jnp.where(is_first, own, other)
        second_ref[n] = jnp.where(is_first, other, own)


def clipped(own, other):
    shape = jax.ShapeDtypeStruct((3, F, F), F32)
    return pl.pallas_call(
        clip_kernel,
        out_shape=[shape, shape],
        compiler_params=pltpu.CompilerParams(vmem_limit_bytes=8 << 20),
        name="clip",
    )(*on_chip(own, other))


def shards(pixels, offsets, first_weights, second_weights, cotangent):
    px = pixels.reshape(R * C, F)
    ct = cotangent.reshape(PR * PC, F)
    up, down, *strips, wide = row_messages(px, ct, offsets)
    above, below = exchanged(up, down, GRP)
    left, right = exchanged(*col_messages(*strips, wide, above, below), DEV)
    got = (above, below, left, right)
    terms, keep, send, table, grad = main_stage(
        px, ct, wide, first_weights, second_weights, got
    )
    own = total_of(keep, send)
    grad_pixels, level = tail_stage(terms, table, grad, first_weights, second_weights)
    own, grad_pixels, level = lax.optimization_barrier((own, grad_pixels, level))
    first, second = clipped(own, swapped(own))
    return grad_pixels.reshape(R, C, F), first, second, level.reshape(PR, PC, F)


def solution(mesh):
    finer = Mesh(mesh.devices.reshape(-1, 2, 4, mesh.devices.shape[1] // 4), EVERY)
    in_specs = (P(GRP, DEV, None), P(GRP, DEV), P(), P(), P(GRP, DEV, None))
    out_specs = (P(GRP, DEV, None), P(), P(), P(GRP, DEV, None))
    return jax.shard_map(
        shards, mesh=finer, in_specs=in_specs, out_specs=out_specs, check_vma=False
    )
```

```python
import functools

import jax
import jax.numpy as jnp
from jax import lax
from jax.experimental import pallas as pl
from jax.experimental.pallas import tpu as pltpu
from jax.sharding import Mesh
from jax.sharding import PartitionSpec as P

GRP = ("grp_0", "grp_1")
DEV = ("dev_0", "dev_1")
EVERY = GRP + DEV
BF = jnp.bfloat16
F32 = jnp.float32

R, C, F = 16, 64, 256
PR, PC = R // 2, C // 2
HR, HC = 6, 8
ER, EC = R + 2 * HR, C + 2 * HC
QR, QC = PR + 6, PC + 8
OR = R + 16

STEPS = (
    (-1, 0, 1.0),
    (1, 0, 1.0),
    (0, -1, 1.0),
    (0, 1, 1.0),
    (-1, -1, 0.5),
    (-1, 1, 0.5),
    (1, -1, 0.5),
    (1, 1, 0.5),
)


def mm(a, b):
    return lax.dot_general(a, b, (((1,), (0,)), ((), ())), preferred_element_type=F32)


def mm_nt(a, b):
    return lax.dot_general(a, b, (((1,), (1,)), ((), ())), preferred_element_type=F32)


def mm_tn(a, b):
    return lax.dot_general(a, b, (((0,), (0,)), ((), ())), preferred_element_type=F32)


ROW_CT = HR * C
ROW_OFF = ROW_CT + 3 * PC
ROW_END = ROW_OFF + 32
COL_CT = ER * HC
COL_OFF = COL_CT + 64
COL_END = COL_OFF + OR


def on_chip(*arrays):
    return [pltpu.with_memory_space_constraint(a, pltpu.VMEM) for a in arrays]


def in_hbm(*arrays):
    return [pltpu.with_memory_space_constraint(a, pltpu.HBM) for a in arrays]


def rolled(x, shift, axis):
    return pltpu.roll(x, shift % x.shape[axis], axis)


def in_parts(x):
    high = x.astype(BF).astype(F32)
    left = x - high
    middle = left.astype(BF).astype(F32)
    return high, middle, left - middle


def started(sems, pairs):
    copies = [pltpu.make_async_copy(src, dst, sems.at[n]) for n, (src, dst) in enumerate(pairs)]
    for copy in copies:
        copy.start()
    return copies


def row_pack_kernel(px_ref, ct_ref, px_rows, ct_rows, off_ref, *rest):
    up_ref, down_ref, pxl_ref, pxr_ref, ctl_ref, ctr_ref, wide, off_buf, sems = rest
    pairs = [(off_ref, off_buf)]
    for out, px_at, ct_at in ((up_ref, 0, 0), (down_ref, R - HR, PR - 3)):
        for ref, at, size, to in ((px_ref, px_at * C, HR * C, 0), (ct_ref, ct_at * PC, 3 * PC, ROW_CT)):
            pairs.append((ref.at[pl.ds(at, size), :], out.at[pl.ds(to, size), :]))
    pairs += [
        (px_rows.at[:, pl.ds(0, 16), :], pxl_ref),
        (px_rows.at[:, pl.ds(C - 16, 16), :], pxr_ref),
        (ct_rows.at[:, pl.ds(0, 16), :], ctl_ref),
        (ct_rows.at[:, pl.ds(PC - 16, 16), :], ctr_ref),
    ]
    copies = started(sems, pairs)
    wide[...] = jnp.zeros_like(wide)
    copies[0].wait()
    wide[:, 0:C] = off_buf[...]
    for out, off_at in ((up_ref, 0), (down_ref, R - 8)):
        high, middle, low = in_parts(wide[off_at : off_at + 8, :])
        packed = jnp.concatenate([high, middle, low, jnp.zeros_like(low)], 0)
        out[ROW_OFF:ROW_END, :] = jnp.concatenate([packed, jnp.zeros_like(packed)], 1).astype(BF)
    for copy in copies[1:]:
        copy.wait()


def row_messages(pixels, cotangent, offsets):
    return pl.pallas_call(
        row_pack_kernel,
        in_specs=[pl.BlockSpec(memory_space=pltpu.HBM)] * 5,
        out_shape=[
            pltpu.VMEM((ROW_END, F), BF),
            pltpu.VMEM((ROW_END, F), BF),
            pltpu.VMEM((R, 16, F), BF),
            pltpu.VMEM((R, 16, F), BF),
            pltpu.VMEM((PR, 16, F), BF),
            pltpu.VMEM((PR, 16, F), BF),
            pltpu.VMEM((R, 128), F32),
        ],
        scratch_shapes=[pltpu.VMEM((R, C), F32), pltpu.SemaphoreType.DMA((9,))],
        compiler_params=pltpu.CompilerParams(vmem_limit_bytes=4 << 20),
        name="row_pack",
    )(*in_hbm(pixels, cotangent, pixels.reshape(R, C, F), cotangent.reshape(PR, PC, F), offsets))


def row_offsets(ref):
    parts = ref[ROW_OFF:ROW_END, 0:128].astype(F32)
    return parts[0:8] + parts[8:16] + parts[16:24]


def col_pack_kernel(*refs):
    pxl_ref, pxr_ref, ctl_ref, ctr_ref, off_ref, above_ref, below_ref, left_ref, right_ref, wide = refs
    wide[8 : 8 + R, :] = off_ref[...]
    wide[0:8, :] = row_offsets(above_ref)
    wide[8 + R : OR, :] = row_offsets(below_ref)
    lane = lax.broadcasted_iota(jnp.int32, (OR, 128), 1)
    near = lax.broadcasted_iota(jnp.int32, (8, F), 0) < 4
    for out, px_ref, ct_ref, px_at, ct_at, half in (
        (left_ref, pxl_ref, ctl_ref, 0, 0, slice(0, 8)),
        (right_ref, pxr_ref, ctr_ref, C - 16, PC - 16, slice(8, 16)),
    ):

        def line(ref, k, base, width, at):
            if ref is above_ref or ref is below_ref:
                return ref[base + k * width + at : base + k * width + at + 16, :].astype(F32)[half]
            return ref[k].astype(F32)[half]

        for first, n, ref in ((0, HR, above_ref), (HR, R, px_ref), (HR + R, HR, below_ref)):
            for r in range(0, n, 2):
                tiles = [line(ref, k, 0, C, px_at) for k in (r, r + 1)]
                at = (first + r) * HC
                out[at : at + 16, :] = jnp.concatenate(tiles, 0).astype(BF)
        lines = []
        for n, ref in ((3, above_ref), (PR, ct_ref), (3, below_ref)):
            lines += [line(ref, k, ROW_CT, PC, ct_at) for k in range(n)]
        tiles = []
        for e in range(0, QR, 2):
            first, second = lines[e], lines[e + 1]
            if out is left_ref:
                second = rolled(second, 4, 0)
            else:
                first = rolled(first, 4, 0)
            tiles.append(jnp.where(near, first, second))
        tiles.append(jnp.zeros((8, F), F32))
        out[COL_CT:COL_OFF, :] = jnp.concatenate(tiles, 0).astype(BF)
        part = wide[...] if out is left_ref else rolled(wide[...], HC - C, 1)
        high, middle, low = in_parts(jnp.where(lane < HC, part, 0.0))
        packed = high + rolled(middle, HC, 1) + rolled(low, 2 * HC, 1)
        out[COL_OFF:COL_END, :] = jnp.concatenate([packed, jnp.zeros_like(packed)], 1).astype(BF)


def col_messages(*parts):
    shape = pltpu.VMEM((COL_END, F), BF)
    return pl.pallas_call(
        col_pack_kernel,
        out_shape=[shape, shape],
        scratch_shapes=[pltpu.VMEM((OR, 128), F32)],
        compiler_params=pltpu.CompilerParams(vmem_limit_bytes=4 << 20),
        name="col_pack",
    )(*on_chip(*parts))


def exchanged(first, last, axis):
    count = lax.axis_size(axis)
    forward = [(i, i + 1) for i in range(count - 1)]
    backward = [(i + 1, i) for i in range(count - 1)]
    return lax.ppermute(last, axis, forward), lax.ppermute(first, axis, backward)


def inverse_roots(h, inside):
    degree = jnp.zeros_like(h)
    edges = {}
    for row_step, col_step, coupling in STEPS:
        other = rolled(rolled(h, row_step, 0), col_step, 1)
        present = rolled(rolled(inside, row_step, 0), col_step, 1)
        edges[row_step, col_step] = jnp.exp(-(h - other) * (h - other))
        degree = degree + coupling * present * edges[row_step, col_step]
    return lax.rsqrt(degree + 1.0 - inside) * inside, edges


def couplings(row_gap, col_gap):
    near = jnp.abs(col_gap)
    side = jnp.where(near == 0, 1.0, jnp.where(near == 1, 0.5, 0.0))
    own = jnp.where(near == 1, 1.0, 0.0)
    return jnp.where(row_gap == 0, own, jnp.where(jnp.abs(row_gap) == 1, side, 0.0))


def fine_windows(above, own, below):
    lane = lax.broadcasted_iota(jnp.int32, own.shape, 1)
    over = rolled(own, EC, 1)
    low = jnp.where(lane < EC, rolled(above, 1, 0), over)
    high = jnp.where(lane < 2 * EC - 128, over, rolled(rolled(below, -1, 0), 2 * EC - 128, 1))
    return jnp.concatenate([low, high], 1)


def pooled_windows(x):
    lane = lax.broadcasted_iota(jnp.int32, x.shape, 1)
    rows = [rolled(rolled(x, 1 - j, 0), QC * j, 1) for j in range(6)]
    low = jnp.where(
        lane < QC,
        rows[0],
        jnp.where(lane < 2 * QC, rows[1], jnp.where(lane < 3 * QC, rows[2], rows[3])),
    )
    high = jnp.where(
        lane < 4 * QC - 128,
        rows[3],
        jnp.where(
            lane < 5 * QC - 128, rows[4], jnp.where(lane < 6 * QC - 128, rows[5], 0.0)
        ),
    )
    return jnp.concatenate([low, high], 1)


def in_two(x):
    high = x.astype(BF)
    return jnp.concatenate([high, (x - high.astype(F32)).astype(BF)], 0)


def applied(table, values):
    both = mm(table, values)
    half = both.shape[0] // 2
    return both[0:half] + both[half:]


def transposed(x):
    if x.shape[0] < 128:
        x = jnp.concatenate([x, jnp.zeros((128 - x.shape[0], 128), F32)], 0)
    return x.T


def main_kernel(px_hbm, ct_hbm, w1_hbm, w2_hbm, off_ref, above_ref, below_ref, left_ref, right_ref, *rest):
    terms_hbm, keep_ref, send_ref, table_ref, grad_hbm = rest[:5]
    (h_ref, hw_ref, pick_ref, phw_ref, psw_ref, pxe_ref, f1_ref, f2_ref, f1c_ref, f2c_ref, slope_ref, hid_ref,
     poolf_ref, p1f_ref, p2f_ref, ctf_ref, ptab_ref, pb_ref, p1b_ref, ctb_ref, topb_ref,
     midf_ref, midb_ref, pgf_ref, sp_ref, agc_ref, halves_ref, px_ref, ct_ref, w1_ref, w2_ref,
     terms_ref, grad_ref, pxt_ref, f1t_ref, f2t_ref, sems, out_sems) = rest[5:]
    copies = started(
        sems, [(px_hbm, px_ref), (ct_hbm, ct_ref), (w1_hbm, w1_ref), (w2_hbm, w2_ref)]
    )
    core = lax.axis_index("grp_1")

    row0 = (lax.axis_index("grp_0") * 2 + lax.axis_index("grp_1")) * R
    col0 = (lax.axis_index("dev_0") * lax.axis_size("dev_1") + lax.axis_index("dev_1")) * C
    rows_all = lax.axis_size("grp_0") * lax.axis_size("grp_1") * R
    cols_all = lax.axis_size("dev_0") * lax.axis_size("dev_1") * C

    h_ref[8 : 8 + R, :] = off_ref[...]
    h_ref[0:8, :] = row_offsets(above_ref)
    h_ref[8 + R : OR, :] = row_offsets(below_ref)

    def col_offsets(ref):
        parts = ref[COL_OFF:COL_END, 0:128].astype(F32)
        whole = parts + rolled(parts, -HC, 1) + rolled(parts, -2 * HC, 1)
        return jnp.where(lax.broadcasted_iota(jnp.int32, (OR, 128), 1) < HC, whole, 0.0)

    h_ref[...] = (
        col_offsets(left_ref) + rolled(h_ref[...], HC, 1) + rolled(col_offsets(right_ref), HC + C, 1)
    )
    h = h_ref[...]
    q = lax.broadcasted_iota(jnp.int32, (OR, 128), 0)
    c = lax.broadcasted_iota(jnp.int32, (OR, 128), 1)
    row_id = row0 - 8 + q
    col_id = col0 - HC + c
    inside = (
        (row_id >= 0) & (row_id < rows_all) & (col_id >= 0) & (col_id < cols_all) & (c < EC)
    ).astype(F32)
    s, edges = inverse_roots(h, inside)

    pick_r = lax.broadcasted_iota(jnp.int32, (OR // 2, OR), 1) // 2
    pick_r = jnp.where(pick_r == lax.broadcasted_iota(jnp.int32, (OR // 2, OR), 0), 0.5, 0.0)
    pick_c = lax.broadcasted_iota(jnp.int32, (128, 128), 0) // 2
    pick_c = jnp.where(pick_c == lax.broadcasted_iota(jnp.int32, (128, 128), 1), 0.5, 0.0)
    ph = jnp.dot(pick_r, h, precision=lax.Precision.HIGHEST, preferred_element_type=F32)
    ph = jnp.dot(ph, pick_c, precision=lax.Precision.HIGHEST, preferred_element_type=F32)
    pq = lax.broadcasted_iota(jnp.int32, (OR // 2, 128), 0)
    pc = lax.broadcasted_iota(jnp.int32, (OR // 2, 128), 1)
    prow = row0 // 2 - 4 + pq
    pcol = col0 // 2 - 4 + pc
    pinside = (
        (prow >= 0) & (prow < rows_all // 2) & (pcol >= 0) & (pcol < cols_all // 2) & (pc < QC)
    ).astype(F32)
    ps, _ = inverse_roots(ph, pinside)

    k = lax.broadcasted_iota(jnp.int32, (EC, 256), 1)
    i = lax.broadcasted_iota(jnp.int32, (EC, 256), 0)
    block = (k >= EC).astype(jnp.int32) + (k >= 2 * EC).astype(jnp.int32)
    gap = jnp.where(k < 3 * EC, k - block * EC - i, 9)
    for n, col_step in enumerate((-1, 0, 1)):
        parts = []
        for row_step in (-1, 0, 1):
            if (row_step, col_step) == (0, 0):
                parts.append(jnp.zeros_like(h))
                continue
            coupling = 0.5 if row_step and col_step else 1.0
            other = rolled(rolled(s, row_step, 0), col_step, 1)
            parts.append(-coupling * edges[row_step, col_step] * (s * other))
        window = fine_windows(*parts)
        high = window.astype(BF).astype(F32)
        hw_ref[n] = high
        hw_ref[3 + n] = window - high
        pick_ref[n] = jnp.where(gap == col_step, 1.0, 0.0).astype(BF)
    for r in range(1, ER - 1):
        at = r + 2
        for part in (0, 1):
            lines = []
            for n in range(3):
                line = hw_ref[3 * part + n, at : at + 1, :]
                lines.append(jnp.broadcast_to(line, (16, 256)).astype(BF))
            base = (2 * (r - 1) + part) * EC
            for t in range(0, EC, 16):
                picked = pick_ref[0, t : t + 16, :] * lines[0]
                picked = picked + pick_ref[1, t : t + 16, :] * lines[1]
                picked = picked + pick_ref[2, t : t + 16, :] * lines[2]
                table_ref[base + t : base + t + 16, :] = picked
    phw_ref[...] = pooled_windows(ph)
    psw_ref[...] = pooled_windows(ps)
    pht, pst = transposed(ph), transposed(ps)
    k = lax.broadcasted_iota(jnp.int32, (QC, 256), 1)
    i = lax.broadcasted_iota(jnp.int32, (QC, 256), 0)
    block = sum((k >= QC * j).astype(jnp.int32) for j in range(1, 6))
    plinks = [-couplings(block - 1 - j, k - block * QC - i) for j in range(4)]
    for b in range(3):
        at = 2 + 4 * b
        for j in (0, 2):
            both = []
            for jj in (j, j + 1):
                col = at + jj
                gap = pht[0:QC, col : col + 1] - phw_ref[at : at + 1, :]
                scale = pst[0:QC, col : col + 1] * psw_ref[at : at + 1, :]
                both.append(plinks[jj] * jnp.exp(-gap * gap) * scale)
            two = in_two(jnp.concatenate(both, 0))
            at_row = 2 * b * 160 + j * QC
            ptab_ref[at_row : at_row + 2 * QC, :] = two[0 : 2 * QC]
            ptab_ref[at_row + 160 : at_row + 160 + 2 * QC, :] = two[2 * QC :]

    copies[0].wait()
    copies[1].wait()
    for at, n, ref in ((0, HR, above_ref), (HR, R, px_ref), (HR + R, HR, below_ref)):
        for r in range(0, n, 2):
            side = slice((at + r) * HC, (at + r + 2) * HC)
            left, right = left_ref[side, :].astype(F32), right_ref[side, :].astype(F32)
            middle = ref[r * C : (r + 2) * C, :].astype(F32)
            lines = [left[0:8], middle[0:C], right[0:8], left[8:16], middle[C:], right[8:16]]
            row = (at + r) * EC
            pxe_ref[row : row + 2 * EC, :] = jnp.concatenate(lines, 0).astype(BF)

    left = left_ref[COL_CT:COL_OFF, :].astype(F32)
    right = right_ref[COL_CT:COL_OFF, :].astype(F32)
    for at, n, base, ref in ((0, 3, ROW_CT, above_ref), (3, PR, 0, ct_ref), (3 + PR, 3, ROW_CT, below_ref)):
        for r in range(n):
            e = at + r
            ctf_ref[e * QC : e * QC + 4, :] = left[e * 4 : e * 4 + 4]
            ctf_ref[e * QC + 4 : e * QC + 4 + PC, :] = ref[base + r * PC : base + (r + 1) * PC, :].astype(F32)
            ctf_ref[e * QC + 4 + PC : (e + 1) * QC, :] = right[e * 4 : e * 4 + 4]
    ctb_ref[...] = ctf_ref[...].astype(BF)

    copies[2].wait()
    copies[3].wait()

    def table_of(r):
        return table_ref[2 * (r - 1) * EC : 2 * r * EC, 0 : 3 * EC]

    def turn(ref, to_ref, n):
        to_ref[:, n * 128 : (n + 1) * 128] = ref[n * 128 : (n + 1) * 128, :].T

    for r in range(1, ER - 1):
        if 4 <= r < 20 and r % 2 == 0:
            turn(px_ref, pxt_ref, (r - 4) // 2)
        one = applied(table_of(r), pxe_ref[(r - 1) * EC : (r + 2) * EC, :])
        f1_ref[(r - 1) * EC : r * EC, :] = one.astype(BF)
        if HR <= r < HR + R:
            f1c_ref[(r - HR) * C : (r - HR + 1) * C, :] = one[HC : HC + C].astype(BF)
    for r in range(2, ER - 2):
        if 4 <= r < 20 and r % 2 == 0:
            turn(f1c_ref, f1t_ref, (r - 4) // 2)
        two = 2.0 * applied(table_of(r), f1_ref[(r - 2) * EC : (r + 1) * EC, :])
        two = two - pxe_ref[r * EC : (r + 1) * EC, :].astype(F32)
        f2_ref[(r - 2) * EC : (r - 1) * EC, :] = two.astype(BF)
        if HR <= r < HR + R:
            f2c_ref[(r - HR) * C : (r - HR + 1) * C, :] = two[HC : HC + C].astype(BF)
    poolf_ref[...] = jnp.zeros_like(poolf_ref)
    p1f_ref[...] = jnp.zeros_like(p1f_ref)
    midf_ref[...] = jnp.zeros_like(midf_ref)
    for b in range(6):
        r = 2 + 4 * b
        terms = [
            pxe_ref[r * EC : (r + 4) * EC, :],
            f1_ref[(r - 1) * EC : (r + 3) * EC, :],
            f2_ref[(r - 2) * EC : (r + 2) * EC, :],
        ]
        act = mm(jnp.concatenate(terms, 1), w1_ref[...].reshape(3 * F, F))
        sig = 0.5 * jnp.tanh(0.5 * act) + 0.5
        hid = act * sig
        slope_ref[(r - 2) * EC : (r + 2) * EC, :] = sig + hid * (1.0 - sig)
        for n in ((0, 1), (2, 3), (4,), (5,), (6,), (7,))[b]:
            turn(f2c_ref, f2t_ref, n)
        for n in (0, 1):
            half = hid[:, n * 128 : (n + 1) * 128]
            ref = hid_ref.at[2 * b + n]
            ref[0:EC, :] = half[0:EC] + half[EC : 2 * EC]
            ref[EC : 2 * EC, :] = half[2 * EC : 3 * EC] + half[3 * EC : 4 * EC]
            pooled = 0.25 * (ref[pl.ds(0, EC, stride=2), :] + ref[pl.ds(1, EC, stride=2), :])
            pooled = pooled.astype(BF).astype(F32)
            poolf_ref[(1 + 2 * b) * QC : (3 + 2 * b) * QC, n * 128 : (n + 1) * 128] = pooled
    pb_ref[...] = poolf_ref[...].astype(BF)

    def ptable_of(b):
        return ptab_ref[b * 320 : (b + 1) * 320, 0 : 6 * QC]

    for b in range(3):
        one = applied(ptable_of(b), pb_ref[b * 160 : b * 160 + 6 * QC, :])
        p1f_ref[(1 + 4 * b) * QC : (5 + 4 * b) * QC, :] = one
    p1b_ref[...] = p1f_ref[...].astype(BF)
    for b in range(3):
        two = 2.0 * applied(ptable_of(b), p1b_ref[b * 160 : b * 160 + 6 * QC, :])
        lines = slice((1 + 4 * b) * QC, (5 + 4 * b) * QC)
        p2f_ref[lines, :] = two - poolf_ref[lines, :]
    own = slice(3 * QC, 11 * QC)
    terms = [poolf_ref[own, :].astype(BF), p1f_ref[own, :].astype(BF), p2f_ref[own, :].astype(BF)]
    for n, term in enumerate(terms):
        terms_ref[n] = term
    outward = [pltpu.make_async_copy(terms_ref, terms_hbm, out_sems.at[0])]
    outward[0].start()
    col = lax.broadcasted_iota(jnp.int32, (QC, F), 0)
    keep = ((col >= 4) & (col < 4 + PC)).astype(F32)
    cot_own = (ctf_ref[own, :].reshape(PR, QC, F) * keep[None]).reshape(PR * QC, F).astype(BF)
    for n, term in enumerate(terms):
        halves_ref[1 - core, n * F : (n + 1) * F, :] = mm_tn(term, cot_own).astype(BF)

    cot = ctb_ref[...]
    topb_ref[...] = mm_nt(cot, w2_ref[2]).astype(BF)
    from_one = mm_nt(cot, w2_ref[1])
    for b in range(3):
        lines = slice((1 + 4 * b) * QC, (5 + 4 * b) * QC)
        mid = 2.0 * applied(ptable_of(b), topb_ref[b * 160 : b * 160 + 6 * QC, :])
        midf_ref[lines, :] = from_one[lines] + mid
    midb_ref[...] = midf_ref[...].astype(BF)
    from_zero = mm_nt(cot, w2_ref[0]) - topb_ref[...].astype(F32)
    for b in range(3):
        lines = slice((1 + 4 * b) * QC, (5 + 4 * b) * QC)
        pgf_ref[lines, :] = from_zero[lines] + applied(ptable_of(b), midb_ref[b * 160 : b * 160 + 6 * QC, :])
    for b in range(5):
        u = 2 + 2 * b
        grad = 0.25 * pgf_ref[u * QC : (u + 2) * QC, :]
        for n in (0, 1):
            ref = sp_ref.at[2 * b + n]
            ref[pl.ds(0, 2 * QC, stride=2), :] = grad[:, n * 128 : (n + 1) * 128]
            ref[pl.ds(1, 2 * QC, stride=2), :] = grad[:, n * 128 : (n + 1) * 128]
        for n in range(4):
            r = 2 * u + n
            lines = slice((n // 2) * EC, (n // 2 + 1) * EC)
            spread = jnp.concatenate([sp_ref[2 * b, lines, :], sp_ref[2 * b + 1, lines, :]], 1)
            grad_row = spread * slope_ref[(r - 2) * EC : (r - 1) * EC, :]
            grad_ref[(r - 4) * EC : (r - 3) * EC, :] = grad_row.astype(BF)
            if HR <= r < HR + R:
                agc_ref[(r - HR) * C : (r - HR + 1) * C, :] = grad_row[HC : HC + C].astype(BF)
    outward.append(pltpu.make_async_copy(grad_ref, grad_hbm, out_sems.at[1]))
    outward[1].start()
    for n, ref in enumerate((pxt_ref, f1t_ref, f2t_ref)):
        halves_ref[core, n * F : (n + 1) * F, :] = mm(ref[...], agc_ref[...]).astype(BF)
    keep_ref[...] = halves_ref[0]
    send_ref[...] = halves_ref[1]
    for copy in outward:
        copy.wait()


def main_stage(pixels, cotangent, offsets, first_weights, second_weights, got):
    fine, pooled = ER * EC, QR * QC
    scratch = [
        ((OR, 128), F32),
        ((6, OR, 256), F32),
        ((3, EC, 256), BF),
        ((OR // 2, 256), F32),
        ((OR // 2, 256), F32),
        ((fine, F), BF),
        ((26 * EC, F), BF),
        ((24 * EC, F), BF),
        ((R * C, F), BF),
        ((R * C, F), BF),
        ((24 * EC, F), F32),
        ((12, 2 * EC, 128), F32),
        ((pooled, F), F32),
        ((pooled, F), F32),
        ((pooled, F), F32),
        ((pooled, F), F32),
        ((960, 256), BF),
        ((pooled, F), BF),
        ((pooled, F), BF),
        ((pooled, F), BF),
        ((pooled, F), BF),
        ((pooled, F), F32),
        ((pooled, F), BF),
        ((pooled, F), F32),
        ((10, 2 * EC, 128), F32),
        ((R * C, F), BF),
        ((2, 3 * F, F), BF),
        ((R * C, F), BF),
        ((PR * PC, F), BF),
        ((3, F, F), BF),
        ((3, F, F), BF),
        ((3, PR * QC, F), BF),
        ((20 * EC, F), BF),
        ((F, R * C), BF),
        ((F, R * C), BF),
        ((F, R * C), BF),
    ]
    return pl.pallas_call(
        main_kernel,
        out_shape=[
            pltpu.HBM((3, PR * QC, F), BF),
            pltpu.VMEM((3 * F, F), BF),
            pltpu.VMEM((3 * F, F), BF),
            pltpu.VMEM((52 * EC, 256), BF),
            pltpu.HBM((20 * EC, F), BF),
        ],
        in_specs=[pl.BlockSpec(memory_space=pl.ANY)] * 4
        + [pl.BlockSpec(memory_space=pltpu.VMEM)] * 5,
        scratch_shapes=[pltpu.VMEM(shape, dtype) for shape, dtype in scratch]
        + [pltpu.SemaphoreType.DMA((4,)), pltpu.SemaphoreType.DMA((2,))],
        compiler_params=pltpu.CompilerParams(vmem_limit_bytes=20 << 20),
        name="main",
    )(pixels, cotangent, first_weights, second_weights, *on_chip(offsets, *got))


def tail_kernel(terms_ref, table_ref, grad_ref, w_ref, w2_ref, out_ref, level_ref, top_ref, mid_ref, low_ref):
    top_ref[...] = mm_nt(grad_ref[...], w_ref[2]).astype(BF)
    for b in range(9):
        r = 5 + 2 * b
        base = mm_nt(grad_ref[(r - 4) * EC : (r - 2) * EC, :], w_ref[1])
        for n in (0, 1):
            table = table_ref[2 * (r + n - 1) * EC : 2 * (r + n) * EC, 0 : 3 * EC]
            mid = 2.0 * applied(table, top_ref[(r + n - 5) * EC : (r + n - 2) * EC, :])
            mid = base[n * EC : (n + 1) * EC] + mid
            mid_ref[(r + n - 5) * EC : (r + n - 4) * EC, :] = mid.astype(BF)
    for b in range(8):
        r = 6 + 2 * b
        base = mm_nt(grad_ref[(r - 4) * EC : (r - 2) * EC, :], w_ref[0])
        base = base - top_ref[(r - 4) * EC : (r - 2) * EC, :].astype(F32)
        for n in (0, 1):
            table = table_ref[2 * (r + n - 1) * EC : 2 * (r + n) * EC, 0 : 3 * EC]
            line = base[n * EC : (n + 1) * EC] + applied(table, mid_ref[(r + n - 6) * EC : (r + n - 3) * EC, :])
            at = (r + n - HR) * C
            out_ref[at : at + C, :] = line[HC : HC + C].astype(BF)
    low_ref[...] = sum(mm(terms_ref[n], w2_ref[n]) for n in range(3))
    for r in range(PR):
        level_ref[r * PC : (r + 1) * PC, :] = low_ref[r * QC + 4 : r * QC + 4 + PC, :].astype(BF)


def tail_stage(terms, table, grad, first_weights, second_weights):
    return pl.pallas_call(
        tail_kernel,
        out_shape=[
            jax.ShapeDtypeStruct((R * C, F), BF),
            jax.ShapeDtypeStruct((PR * PC, F), BF),
        ],
        scratch_shapes=[
            pltpu.VMEM((20 * EC, F), BF),
            pltpu.VMEM((18 * EC, F), BF),
            pltpu.VMEM((PR * QC, F), F32),
        ],
        compiler_params=pltpu.CompilerParams(vmem_limit_bytes=8 << 20),
        name="tail",
    )(*in_hbm(terms), *on_chip(table), *in_hbm(grad), first_weights, second_weights)


def sum_at_owner(value, axes):
    tiles = lax.all_to_all(value.reshape(lax.axis_size(axes), -1, F), axes, 0, 0, tiled=True)
    return jnp.sum(tiles.astype(F32), axis=0).astype(BF)


def sent_to_all(value, axes):
    copies = jnp.broadcast_to(value, (lax.axis_size(axes), *value.shape))
    return lax.all_to_all(copies, axes, 0, 0, tiled=True)


def swapped(value):
    return lax.ppermute(value, "grp_1", [(0, 1), (1, 0)])


def total_of(keep, send):
    value = (keep.astype(F32) + swapped(send).astype(F32)).astype(BF)
    value = sum_at_owner(value, DEV)
    value = jnp.sum(sent_to_all(value, ("grp_0",)).astype(F32), axis=0).astype(BF)
    return sent_to_all(value, DEV).reshape(-1, F)


def clip_kernel(own_ref, other_ref, first_ref, second_ref):
    total = jnp.zeros((8, F), F32)
    for ref in (own_ref, other_ref):
        for n in range(3):
            part = ref[n * F : (n + 1) * F, :].astype(F32)
            total = total + jnp.sum((part * part).reshape(F // 8, 8, F), axis=0)
    square_sum = jnp.sum(jnp.sum(total, axis=1, keepdims=True), axis=0, keepdims=True)
    factor = jnp.minimum(1.0, 2.0 * F * lax.rsqrt(square_sum + 1e-06))
    is_first = lax.axis_index("grp_1") == 0
    for n in range(3):
        own = own_ref[n * F : (n + 1) * F, :].astype(F32) * factor
        other = other_ref[n * F : (n + 1) * F, :].astype(F32) * factor
        first_ref[n] = jnp.where(is_first, own, other)
        second_ref[n] = jnp.where(is_first, other, own)


def clipped(own, other):
    shape = jax.ShapeDtypeStruct((3, F, F), F32)
    return pl.pallas_call(
        clip_kernel,
        out_shape=[shape, shape],
        compiler_params=pltpu.CompilerParams(vmem_limit_bytes=8 << 20),
        name="clip",
    )(*on_chip(own, other))


def shards(pixels, offsets, first_weights, second_weights, cotangent):
    px = pixels.reshape(R * C, F)
    ct = cotangent.reshape(PR * PC, F)
    up, down, *strips, wide = row_messages(px, ct, offsets)
    above, below = exchanged(up, down, GRP)
    left, right = exchanged(*col_messages(*strips, wide, above, below), DEV)
    got = (above, below, left, right)
    terms, keep, send, table, grad = main_stage(
        px, ct, wide, first_weights, second_weights, got
    )
    own = total_of(keep, send)
    grad_pixels, level = tail_stage(terms, table, grad, first_weights, second_weights)
    own, grad_pixels, level = lax.optimization_barrier((own, grad_pixels, level))
    first, second = clipped(own, swapped(own))
    return grad_pixels.reshape(R, C, F), first, second, level.reshape(PR, PC, F)


def solution(mesh):
    finer = Mesh(mesh.devices.reshape(-1, 2, 4, mesh.devices.shape[1] // 4), EVERY)
    in_specs = (P(GRP, DEV, None), P(GRP, DEV), P(), P(), P(GRP, DEV, None))
    out_specs = (P(GRP, DEV, None), P(), P(), P(GRP, DEV, None))
    return jax.shard_map(
        shards, mesh=finer, in_specs=in_specs, out_specs=out_specs, check_vma=False
    )
```

```python
import functools

import jax
import jax.numpy as jnp
from jax import lax
from jax.experimental import pallas as pl
from jax.experimental.pallas import tpu as pltpu
from jax.sharding import Mesh
from jax.sharding import PartitionSpec as P

GRP = ("grp_0", "grp_1")
DEV = ("dev_0", "dev_1")
EVERY = GRP + DEV
BF = jnp.bfloat16
F32 = jnp.float32

R, C, F = 16, 64, 256
PR, PC = R // 2, C // 2
HR, HC = 6, 8
ER, EC = R + 2 * HR, C + 2 * HC
QR, QC = PR + 6, PC + 8
OR = R + 16

STEPS = (
    (-1, 0, 1.0),
    (1, 0, 1.0),
    (0, -1, 1.0),
    (0, 1, 1.0),
    (-1, -1, 0.5),
    (-1, 1, 0.5),
    (1, -1, 0.5),
    (1, 1, 0.5),
)


def mm(a, b):
    return lax.dot_general(a, b, (((1,), (0,)), ((), ())), preferred_element_type=F32)


def mm_nt(a, b):
    return lax.dot_general(a, b, (((1,), (1,)), ((), ())), preferred_element_type=F32)


def mm_tn(a, b):
    return lax.dot_general(a, b, (((0,), (0,)), ((), ())), preferred_element_type=F32)


ROW_CT = HR * C
ROW_OFF = ROW_CT + 3 * PC
ROW_END = ROW_OFF + 32
COL_CT = ER * HC
COL_OFF = COL_CT + 64
COL_END = COL_OFF + OR


def on_chip(*arrays):
    return [pltpu.with_memory_space_constraint(a, pltpu.VMEM) for a in arrays]


def in_hbm(*arrays):
    return [pltpu.with_memory_space_constraint(a, pltpu.HBM) for a in arrays]


def rolled(x, shift, axis):
    return pltpu.roll(x, shift % x.shape[axis], axis)


def in_parts(x):
    high = x.astype(BF).astype(F32)
    left = x - high
    middle = left.astype(BF).astype(F32)
    return high, middle, left - middle


def started(sems, pairs):
    copies = [pltpu.make_async_copy(src, dst, sems.at[n]) for n, (src, dst) in enumerate(pairs)]
    for copy in copies:
        copy.start()
    return copies


def row_pack_kernel(px_ref, ct_ref, px_rows, ct_rows, off_ref, *rest):
    chip_ref, cross_ref, pxl_ref, pxr_ref, ctl_ref, ctr_ref, wide, off_buf, sems = rest
    core = lax.axis_index("grp_1")
    ends = ((chip_ref, 1 - core), (cross_ref, core))
    pairs = [(off_ref, off_buf)]
    for out, low_end in ends:
        px_at = pl.multiple_of(low_end * ((R - HR) * C), 64)
        ct_at = pl.multiple_of(low_end * ((PR - 3) * PC), 32)
        for ref, at, size, to in ((px_ref, px_at, HR * C, 0), (ct_ref, ct_at, 3 * PC, ROW_CT)):
            pairs.append((ref.at[pl.ds(at, size), :], out.at[pl.ds(to, size), :]))
    pairs += [
        (px_rows.at[:, pl.ds(0, 16), :], pxl_ref),
        (px_rows.at[:, pl.ds(C - 16, 16), :], pxr_ref),
        (ct_rows.at[:, pl.ds(0, 16), :], ctl_ref),
        (ct_rows.at[:, pl.ds(PC - 16, 16), :], ctr_ref),
    ]
    copies = started(sems, pairs)
    wide[...] = jnp.zeros_like(wide)
    copies[0].wait()
    wide[:, 0:C] = off_buf[...]
    for out, low_end in ends:
        high, middle, low = in_parts(wide[pl.ds(pl.multiple_of(low_end * (R - 8), 8), 8), :])
        packed = jnp.concatenate([high, middle, low, jnp.zeros_like(low)], 0)
        out[ROW_OFF:ROW_END, :] = jnp.concatenate([packed, jnp.zeros_like(packed)], 1).astype(BF)
    for copy in copies[1:]:
        copy.wait()


def row_messages(pixels, cotangent, offsets):
    return pl.pallas_call(
        row_pack_kernel,
        in_specs=[pl.BlockSpec(memory_space=pltpu.HBM)] * 5,
        out_shape=[
            pltpu.VMEM((ROW_END, F), BF),
            pltpu.VMEM((ROW_END, F), BF),
            pltpu.VMEM((R, 16, F), BF),
            pltpu.VMEM((R, 16, F), BF),
            pltpu.VMEM((PR, 16, F), BF),
            pltpu.VMEM((PR, 16, F), BF),
            pltpu.VMEM((R, 128), F32),
        ],
        scratch_shapes=[pltpu.VMEM((R, C), F32), pltpu.SemaphoreType.DMA((9,))],
        compiler_params=pltpu.CompilerParams(vmem_limit_bytes=4 << 20),
        name="row_pack",
    )(*in_hbm(pixels, cotangent, pixels.reshape(R, C, F), cotangent.reshape(PR, PC, F), offsets))


def row_offsets(ref):
    parts = ref[ROW_OFF:ROW_END, 0:128].astype(F32)
    return parts[0:8] + parts[8:16] + parts[16:24]


def col_pack_kernel(*refs):
    pxl_ref, pxr_ref, ctl_ref, ctr_ref, off_ref, chip_ref, cross_ref = refs[:7]
    first_ref, second_ref, rows_ref, wide, sides = refs[7:]
    core = lax.axis_index("grp_1")
    rows_ref[1 - core] = chip_ref[...]
    rows_ref[core] = cross_ref[...]
    above_ref, below_ref = rows_ref.at[0], rows_ref.at[1]
    odd = column_parity()
    wide[8 : 8 + R, :] = off_ref[...]
    wide[0:8, :] = row_offsets(above_ref)
    wide[8 + R : OR, :] = row_offsets(below_ref)
    lane = lax.broadcasted_iota(jnp.int32, (OR, 128), 1)
    near = lax.broadcasted_iota(jnp.int32, (8, F), 0) < 4
    for is_left, out, px_ref, ct_ref, px_at, ct_at, half in (
        (True, sides.at[1 - odd], pxl_ref, ctl_ref, 0, 0, slice(0, 8)),
        (False, sides.at[odd], pxr_ref, ctr_ref, C - 16, PC - 16, slice(8, 16)),
    ):

        def line(ref, k, base, width, at):
            if len(ref.shape) == 2:
                return ref[base + k * width + at : base + k * width + at + 16, :].astype(F32)[half]
            return ref[k].astype(F32)[half]

        for first, n, ref in ((0, HR, above_ref), (HR, R, px_ref), (HR + R, HR, below_ref)):
            for r in range(0, n, 2):
                tiles = [line(ref, k, 0, C, px_at) for k in (r, r + 1)]
                at = (first + r) * HC
                out[at : at + 16, :] = jnp.concatenate(tiles, 0).astype(BF)
        lines = []
        for n, ref in ((3, above_ref), (PR, ct_ref), (3, below_ref)):
            lines += [line(ref, k, ROW_CT, PC, ct_at) for k in range(n)]
        tiles = []
        for e in range(0, QR, 2):
            first, second = lines[e], lines[e + 1]
            if is_left:
                second = rolled(second, 4, 0)
            else:
                first = rolled(first, 4, 0)
            tiles.append(jnp.where(near, first, second))
        tiles.append(jnp.zeros((8, F), F32))
        out[COL_CT:COL_OFF, :] = jnp.concatenate(tiles, 0).astype(BF)
        part = wide[...] if is_left else rolled(wide[...], HC - C, 1)
        high, middle, low = in_parts(jnp.where(lane < HC, part, 0.0))
        packed = high + rolled(middle, HC, 1) + rolled(low, 2 * HC, 1)
        out[COL_OFF:COL_END, :] = jnp.concatenate([packed, jnp.zeros_like(packed)], 1).astype(BF)
    first_ref[...] = sides[0]
    second_ref[...] = sides[1]


def column_parity():
    return (lax.axis_index("dev_0") * lax.axis_size("dev_1") + lax.axis_index("dev_1")) % 2


def col_messages(*parts):
    shape = pltpu.VMEM((COL_END, F), BF)
    return pl.pallas_call(
        col_pack_kernel,
        out_shape=[shape, shape, pltpu.VMEM((2, ROW_END, F), BF)],
        scratch_shapes=[pltpu.VMEM((OR, 128), F32), pltpu.VMEM((2, COL_END, F), BF)],
        compiler_params=pltpu.CompilerParams(vmem_limit_bytes=4 << 20),
        name="col_pack",
    )(*on_chip(*parts))


def paired(message, axis, start):
    pairs = []
    for i in range(start, lax.axis_size(axis) - 1, 2):
        pairs += [(i, i + 1), (i + 1, i)]
    return lax.ppermute(message, axis, pairs)


def inverse_roots(h, inside):
    degree = jnp.zeros_like(h)
    edges = {}
    for row_step, col_step, coupling in STEPS:
        other = rolled(rolled(h, row_step, 0), col_step, 1)
        present = rolled(rolled(inside, row_step, 0), col_step, 1)
        edges[row_step, col_step] = jnp.exp(-(h - other) * (h - other))
        degree = degree + coupling * present * edges[row_step, col_step]
    return lax.rsqrt(degree + 1.0 - inside) * inside, edges


def couplings(row_gap, col_gap):
    near = jnp.abs(col_gap)
    side = jnp.where(near == 0, 1.0, jnp.where(near == 1, 0.5, 0.0))
    own = jnp.where(near == 1, 1.0, 0.0)
    return jnp.where(row_gap == 0, own, jnp.where(jnp.abs(row_gap) == 1, side, 0.0))


def fine_windows(above, own, below):
    lane = lax.broadcasted_iota(jnp.int32, own.shape, 1)
    over = rolled(own, EC, 1)
    low = jnp.where(lane < EC, rolled(above, 1, 0), over)
    high = jnp.where(lane < 2 * EC - 128, over, rolled(rolled(below, -1, 0), 2 * EC - 128, 1))
    return jnp.concatenate([low, high], 1)


def pooled_windows(x):
    lane = lax.broadcasted_iota(jnp.int32, x.shape, 1)
    rows = [rolled(rolled(x, 1 - j, 0), QC * j, 1) for j in range(6)]
    low = jnp.where(
        lane < QC,
        rows[0],
        jnp.where(lane < 2 * QC, rows[1], jnp.where(lane < 3 * QC, rows[2], rows[3])),
    )
    high = jnp.where(
        lane < 4 * QC - 128,
        rows[3],
        jnp.where(
            lane < 5 * QC - 128, rows[4], jnp.where(lane < 6 * QC - 128, rows[5], 0.0)
        ),
    )
    return jnp.concatenate([low, high], 1)


def in_two(x):
    high = x.astype(BF)
    return jnp.concatenate([high, (x - high.astype(F32)).astype(BF)], 0)


def applied(table, values):
    both = mm(table, values)
    half = both.shape[0] // 2
    return both[0:half] + both[half:]


def transposed(x):
    if x.shape[0] < 128:
        x = jnp.concatenate([x, jnp.zeros((128 - x.shape[0], 128), F32)], 0)
    return x.T


def main_kernel(px_hbm, ct_hbm, w1_hbm, w2_hbm, off_ref, first_ref, second_ref, rows_ref, *rest):
    terms_hbm, keep_ref, send_ref, table_ref, grad_hbm = rest[:5]
    (h_ref, hw_ref, pick_ref, phw_ref, psw_ref, pxe_ref, f1_ref, f2_ref, f1c_ref, f2c_ref, slope_ref, hid_ref,
     poolf_ref, p1f_ref, p2f_ref, ctf_ref, ptab_ref, pb_ref, p1b_ref, ctb_ref, topb_ref,
     midf_ref, midb_ref, pgf_ref, sp_ref, agc_ref, halves_ref, px_ref, ct_ref, w1_ref, w2_ref,
     terms_ref, grad_ref, pxt_ref, f1t_ref, f2t_ref, sides_ref, sems, out_sems) = rest[5:]
    copies = started(
        sems, [(px_hbm, px_ref), (ct_hbm, ct_ref), (w1_hbm, w1_ref), (w2_hbm, w2_ref)]
    )
    core = lax.axis_index("grp_1")
    odd = column_parity()
    sides_ref[1 - odd] = first_ref[...]
    sides_ref[odd] = second_ref[...]
    left_ref, right_ref = sides_ref.at[0], sides_ref.at[1]
    above_ref, below_ref = rows_ref.at[0], rows_ref.at[1]

    row0 = (lax.axis_index("grp_0") * 2 + lax.axis_index("grp_1")) * R
    col0 = (lax.axis_index("dev_0") * lax.axis_size("dev_1") + lax.axis_index("dev_1")) * C
    rows_all = lax.axis_size("grp_0") * lax.axis_size("grp_1") * R
    cols_all = lax.axis_size("dev_0") * lax.axis_size("dev_1") * C

    h_ref[8 : 8 + R, :] = off_ref[...]
    h_ref[0:8, :] = row_offsets(above_ref)
    h_ref[8 + R : OR, :] = row_offsets(below_ref)

    def col_offsets(ref):
        parts = ref[COL_OFF:COL_END, 0:128].astype(F32)
        whole = parts + rolled(parts, -HC, 1) + rolled(parts, -2 * HC, 1)
        return jnp.where(lax.broadcasted_iota(jnp.int32, (OR, 128), 1) < HC, whole, 0.0)

    h_ref[...] = (
        col_offsets(left_ref) + rolled(h_ref[...], HC, 1) + rolled(col_offsets(right_ref), HC + C, 1)
    )
    h = h_ref[...]
    q = lax.broadcasted_iota(jnp.int32, (OR, 128), 0)
    c = lax.broadcasted_iota(jnp.int32, (OR, 128), 1)
    row_id = row0 - 8 + q
    col_id = col0 - HC + c
    inside = (
        (row_id >= 0) & (row_id < rows_all) & (col_id >= 0) & (col_id < cols_all) & (c < EC)
    ).astype(F32)
    s, edges = inverse_roots(h, inside)

    pick_r = lax.broadcasted_iota(jnp.int32, (OR // 2, OR), 1) // 2
    pick_r = jnp.where(pick_r == lax.broadcasted_iota(jnp.int32, (OR // 2, OR), 0), 0.5, 0.0)
    pick_c = lax.broadcasted_iota(jnp.int32, (128, 128), 0) // 2
    pick_c = jnp.where(pick_c == lax.broadcasted_iota(jnp.int32, (128, 128), 1), 0.5, 0.0)
    ph = jnp.dot(pick_r, h, precision=lax.Precision.HIGHEST, preferred_element_type=F32)
    ph = jnp.dot(ph, pick_c, precision=lax.Precision.HIGHEST, preferred_element_type=F32)
    pq = lax.broadcasted_iota(jnp.int32, (OR // 2, 128), 0)
    pc = lax.broadcasted_iota(jnp.int32, (OR // 2, 128), 1)
    prow = row0 // 2 - 4 + pq
    pcol = col0 // 2 - 4 + pc
    pinside = (
        (prow >= 0) & (prow < rows_all // 2) & (pcol >= 0) & (pcol < cols_all // 2) & (pc < QC)
    ).astype(F32)
    ps, _ = inverse_roots(ph, pinside)

    k = lax.broadcasted_iota(jnp.int32, (EC, 256), 1)
    i = lax.broadcasted_iota(jnp.int32, (EC, 256), 0)
    block = (k >= EC).astype(jnp.int32) + (k >= 2 * EC).astype(jnp.int32)
    gap = jnp.where(k < 3 * EC, k - block * EC - i, 9)
    for n, col_step in enumerate((-1, 0, 1)):
        parts = []
        for row_step in (-1, 0, 1):
            if (row_step, col_step) == (0, 0):
                parts.append(jnp.zeros_like(h))
                continue
            coupling = 0.5 if row_step and col_step else 1.0
            other = rolled(rolled(s, row_step, 0), col_step, 1)
            parts.append(-coupling * edges[row_step, col_step] * (s * other))
        window = fine_windows(*parts)
        high = window.astype(BF).astype(F32)
        hw_ref[n] = high
        hw_ref[3 + n] = window - high
        pick_ref[n] = jnp.where(gap == col_step, 1.0, 0.0).astype(BF)
    for r in range(1, ER - 1):
        at = r + 2
        for part in (0, 1):
            lines = []
            for n in range(3):
                line = hw_ref[3 * part + n, at : at + 1, :]
                lines.append(jnp.broadcast_to(line, (16, 256)).astype(BF))
            base = (2 * (r - 1) + part) * EC
            for t in range(0, EC, 16):
                picked = pick_ref[0, t : t + 16, :] * lines[0]
                picked = picked + pick_ref[1, t : t + 16, :] * lines[1]
                picked = picked + pick_ref[2, t : t + 16, :] * lines[2]
                table_ref[base + t : base + t + 16, :] = picked
    phw_ref[...] = pooled_windows(ph)
    psw_ref[...] = pooled_windows(ps)
    pht, pst = transposed(ph), transposed(ps)
    k = lax.broadcasted_iota(jnp.int32, (QC, 256), 1)
    i = lax.broadcasted_iota(jnp.int32, (QC, 256), 0)
    block = sum((k >= QC * j).astype(jnp.int32) for j in range(1, 6))
    plinks = [-couplings(block - 1 - j, k - block * QC - i) for j in range(4)]
    for b in range(3):
        at = 2 + 4 * b
        for j in (0, 2):
            both = []
            for jj in (j, j + 1):
                col = at + jj
                gap = pht[0:QC, col : col + 1] - phw_ref[at : at + 1, :]
                scale = pst[0:QC, col : col + 1] * psw_ref[at : at + 1, :]
                both.append(plinks[jj] * jnp.exp(-gap * gap) * scale)
            two = in_two(jnp.concatenate(both, 0))
            at_row = 2 * b * 160 + j * QC
            ptab_ref[at_row : at_row + 2 * QC, :] = two[0 : 2 * QC]
            ptab_ref[at_row + 160 : at_row + 160 + 2 * QC, :] = two[2 * QC :]

    copies[0].wait()
    copies[1].wait()
    for at, n, ref in ((0, HR, above_ref), (HR, R, px_ref), (HR + R, HR, below_ref)):
        for r in range(0, n, 2):
            side = slice((at + r) * HC, (at + r + 2) * HC)
            left, right = left_ref[side, :].astype(F32), right_ref[side, :].astype(F32)
            middle = ref[r * C : (r + 2) * C, :].astype(F32)
            lines = [left[0:8], middle[0:C], right[0:8], left[8:16], middle[C:], right[8:16]]
            row = (at + r) * EC
            pxe_ref[row : row + 2 * EC, :] = jnp.concatenate(lines, 0).astype(BF)

    left = left_ref[COL_CT:COL_OFF, :].astype(F32)
    right = right_ref[COL_CT:COL_OFF, :].astype(F32)
    for at, n, base, ref in ((0, 3, ROW_CT, above_ref), (3, PR, 0, ct_ref), (3 + PR, 3, ROW_CT, below_ref)):
        for r in range(n):
            e = at + r
            ctf_ref[e * QC : e * QC + 4, :] = left[e * 4 : e * 4 + 4]
            ctf_ref[e * QC + 4 : e * QC + 4 + PC, :] = ref[base + r * PC : base + (r + 1) * PC, :].astype(F32)
            ctf_ref[e * QC + 4 + PC : (e + 1) * QC, :] = right[e * 4 : e * 4 + 4]
    ctb_ref[...] = ctf_ref[...].astype(BF)

    copies[2].wait()
    copies[3].wait()

    def table_of(r):
        return table_ref[2 * (r - 1) * EC : 2 * r * EC, 0 : 3 * EC]

    def turn(ref, to_ref, n):
        to_ref[:, n * 128 : (n + 1) * 128] = ref[n * 128 : (n + 1) * 128, :].T

    for r in range(1, ER - 1):
        if 4 <= r < 20 and r % 2 == 0:
            turn(px_ref, pxt_ref, (r - 4) // 2)
        one = applied(table_of(r), pxe_ref[(r - 1) * EC : (r + 2) * EC, :])
        f1_ref[(r - 1) * EC : r * EC, :] = one.astype(BF)
        if HR <= r < HR + R:
            f1c_ref[(r - HR) * C : (r - HR + 1) * C, :] = one[HC : HC + C].astype(BF)
    for r in range(2, ER - 2):
        if 4 <= r < 20 and r % 2 == 0:
            turn(f1c_ref, f1t_ref, (r - 4) // 2)
        two = 2.0 * applied(table_of(r), f1_ref[(r - 2) * EC : (r + 1) * EC, :])
        two = two - pxe_ref[r * EC : (r + 1) * EC, :].astype(F32)
        f2_ref[(r - 2) * EC : (r - 1) * EC, :] = two.astype(BF)
        if HR <= r < HR + R:
            f2c_ref[(r - HR) * C : (r - HR + 1) * C, :] = two[HC : HC + C].astype(BF)
    poolf_ref[...] = jnp.zeros_like(poolf_ref)
    p1f_ref[...] = jnp.zeros_like(p1f_ref)
    midf_ref[...] = jnp.zeros_like(midf_ref)
    for b in range(6):
        r = 2 + 4 * b
        terms = [
            pxe_ref[r * EC : (r + 4) * EC, :],
            f1_ref[(r - 1) * EC : (r + 3) * EC, :],
            f2_ref[(r - 2) * EC : (r + 2) * EC, :],
        ]
        act = mm(jnp.concatenate(terms, 1), w1_ref[...].reshape(3 * F, F))
        sig = 0.5 * jnp.tanh(0.5 * act) + 0.5
        hid = act * sig
        slope_ref[(r - 2) * EC : (r + 2) * EC, :] = sig + hid * (1.0 - sig)
        for n in ((0, 1), (2, 3), (4,), (5,), (6,), (7,))[b]:
            turn(f2c_ref, f2t_ref, n)
        for n in (0, 1):
            half = hid[:, n * 128 : (n + 1) * 128]
            ref = hid_ref.at[2 * b + n]
            ref[0:EC, :] = half[0:EC] + half[EC : 2 * EC]
            ref[EC : 2 * EC, :] = half[2 * EC : 3 * EC] + half[3 * EC : 4 * EC]
            pooled = 0.25 * (ref[pl.ds(0, EC, stride=2), :] + ref[pl.ds(1, EC, stride=2), :])
            pooled = pooled.astype(BF).astype(F32)
            poolf_ref[(1 + 2 * b) * QC : (3 + 2 * b) * QC, n * 128 : (n + 1) * 128] = pooled
    pb_ref[...] = poolf_ref[...].astype(BF)

    def ptable_of(b):
        return ptab_ref[b * 320 : (b + 1) * 320, 0 : 6 * QC]

    for b in range(3):
        one = applied(ptable_of(b), pb_ref[b * 160 : b * 160 + 6 * QC, :])
        p1f_ref[(1 + 4 * b) * QC : (5 + 4 * b) * QC, :] = one
    p1b_ref[...] = p1f_ref[...].astype(BF)
    for b in range(3):
        two = 2.0 * applied(ptable_of(b), p1b_ref[b * 160 : b * 160 + 6 * QC, :])
        lines = slice((1 + 4 * b) * QC, (5 + 4 * b) * QC)
        p2f_ref[lines, :] = two - poolf_ref[lines, :]
    own = slice(3 * QC, 11 * QC)
    terms = [poolf_ref[own, :].astype(BF), p1f_ref[own, :].astype(BF), p2f_ref[own, :].astype(BF)]
    for n, term in enumerate(terms):
        terms_ref[n] = term
    outward = [pltpu.make_async_copy(terms_ref, terms_hbm, out_sems.at[0])]
    outward[0].start()
    col = lax.broadcasted_iota(jnp.int32, (QC, F), 0)
    keep = ((col >= 4) & (col < 4 + PC)).astype(F32)
    cot_own = (ctf_ref[own, :].reshape(PR, QC, F) * keep[None]).reshape(PR * QC, F).astype(BF)
    for n, term in enumerate(terms):
        halves_ref[1 - core, n * F : (n + 1) * F, :] = mm_tn(term, cot_own).astype(BF)

    cot = ctb_ref[...]
    topb_ref[...] = mm_nt(cot, w2_ref[2]).astype(BF)
    from_one = mm_nt(cot, w2_ref[1])
    for b in range(3):
        lines = slice((1 + 4 * b) * QC, (5 + 4 * b) * QC)
        mid = 2.0 * applied(ptable_of(b), topb_ref[b * 160 : b * 160 + 6 * QC, :])
        midf_ref[lines, :] = from_one[lines] + mid
    midb_ref[...] = midf_ref[...].astype(BF)
    from_zero = mm_nt(cot, w2_ref[0]) - topb_ref[...].astype(F32)
    for b in range(3):
        lines = slice((1 + 4 * b) * QC, (5 + 4 * b) * QC)
        pgf_ref[lines, :] = from_zero[lines] + applied(ptable_of(b), midb_ref[b * 160 : b * 160 + 6 * QC, :])
    for b in range(5):
        u = 2 + 2 * b
        grad = 0.25 * pgf_ref[u * QC : (u + 2) * QC, :]
        for n in (0, 1):
            ref = sp_ref.at[2 * b + n]
            ref[pl.ds(0, 2 * QC, stride=2), :] = grad[:, n * 128 : (n + 1) * 128]
            ref[pl.ds(1, 2 * QC, stride=2), :] = grad[:, n * 128 : (n + 1) * 128]
        for n in range(4):
            r = 2 * u + n
            lines = slice((n // 2) * EC, (n // 2 + 1) * EC)
            spread = jnp.concatenate([sp_ref[2 * b, lines, :], sp_ref[2 * b + 1, lines, :]], 1)
            grad_row = spread * slope_ref[(r - 2) * EC : (r - 1) * EC, :]
            grad_ref[(r - 4) * EC : (r - 3) * EC, :] = grad_row.astype(BF)
            if HR <= r < HR + R:
                agc_ref[(r - HR) * C : (r - HR + 1) * C, :] = grad_row[HC : HC + C].astype(BF)
    outward.append(pltpu.make_async_copy(grad_ref, grad_hbm, out_sems.at[1]))
    outward[1].start()
    for n, ref in enumerate((pxt_ref, f1t_ref, f2t_ref)):
        halves_ref[core, n * F : (n + 1) * F, :] = mm(ref[...], agc_ref[...]).astype(BF)
    keep_ref[...] = halves_ref[0]
    send_ref[...] = halves_ref[1]
    for copy in outward:
        copy.wait()


def main_stage(pixels, cotangent, offsets, first_weights, second_weights, got):
    fine, pooled = ER * EC, QR * QC
    scratch = [
        ((OR, 128), F32),
        ((6, OR, 256), F32),
        ((3, EC, 256), BF),
        ((OR // 2, 256), F32),
        ((OR // 2, 256), F32),
        ((fine, F), BF),
        ((26 * EC, F), BF),
        ((24 * EC, F), BF),
        ((R * C, F), BF),
        ((R * C, F), BF),
        ((24 * EC, F), F32),
        ((12, 2 * EC, 128), F32),
        ((pooled, F), F32),
        ((pooled, F), F32),
        ((pooled, F), F32),
        ((pooled, F), F32),
        ((960, 256), BF),
        ((pooled, F), BF),
        ((pooled, F), BF),
        ((pooled, F), BF),
        ((pooled, F), BF),
        ((pooled, F), F32),
        ((pooled, F), BF),
        ((pooled, F), F32),
        ((10, 2 * EC, 128), F32),
        ((R * C, F), BF),
        ((2, 3 * F, F), BF),
        ((R * C, F), BF),
        ((PR * PC, F), BF),
        ((3, F, F), BF),
        ((3, F, F), BF),
        ((3, PR * QC, F), BF),
        ((20 * EC, F), BF),
        ((F, R * C), BF),
        ((F, R * C), BF),
        ((F, R * C), BF),
        ((2, COL_END, F), BF),
    ]
    return pl.pallas_call(
        main_kernel,
        out_shape=[
            pltpu.HBM((3, PR * QC, F), BF),
            pltpu.VMEM((3 * F, F), BF),
            pltpu.VMEM((3 * F, F), BF),
            pltpu.VMEM((52 * EC, 256), BF),
            pltpu.HBM((20 * EC, F), BF),
        ],
        in_specs=[pl.BlockSpec(memory_space=pl.ANY)] * 4
        + [pl.BlockSpec(memory_space=pltpu.VMEM)] * 4,
        scratch_shapes=[pltpu.VMEM(shape, dtype) for shape, dtype in scratch]
        + [pltpu.SemaphoreType.DMA((4,)), pltpu.SemaphoreType.DMA((2,))],
        compiler_params=pltpu.CompilerParams(vmem_limit_bytes=20 << 20),
        name="main",
    )(pixels, cotangent, first_weights, second_weights, *on_chip(offsets, *got))


def tail_kernel(terms_ref, table_ref, grad_ref, w_ref, w2_ref, out_ref, level_ref, top_ref, mid_ref, low_ref):
    top_ref[...] = mm_nt(grad_ref[...], w_ref[2]).astype(BF)
    for b in range(9):
        r = 5 + 2 * b
        base = mm_nt(grad_ref[(r - 4) * EC : (r - 2) * EC, :], w_ref[1])
        for n in (0, 1):
            table = table_ref[2 * (r + n - 1) * EC : 2 * (r + n) * EC, 0 : 3 * EC]
            mid = 2.0 * applied(table, top_ref[(r + n - 5) * EC : (r + n - 2) * EC, :])
            mid = base[n * EC : (n + 1) * EC] + mid
            mid_ref[(r + n - 5) * EC : (r + n - 4) * EC, :] = mid.astype(BF)
    for b in range(8):
        r = 6 + 2 * b
        base = mm_nt(grad_ref[(r - 4) * EC : (r - 2) * EC, :], w_ref[0])
        base = base - top_ref[(r - 4) * EC : (r - 2) * EC, :].astype(F32)
        for n in (0, 1):
            table = table_ref[2 * (r + n - 1) * EC : 2 * (r + n) * EC, 0 : 3 * EC]
            line = base[n * EC : (n + 1) * EC] + applied(table, mid_ref[(r + n - 6) * EC : (r + n - 3) * EC, :])
            at = (r + n - HR) * C
            out_ref[at : at + C, :] = line[HC : HC + C].astype(BF)
    low_ref[...] = sum(mm(terms_ref[n], w2_ref[n]) for n in range(3))
    for r in range(PR):
        level_ref[r * PC : (r + 1) * PC, :] = low_ref[r * QC + 4 : r * QC + 4 + PC, :].astype(BF)


def tail_stage(terms, table, grad, first_weights, second_weights):
    return pl.pallas_call(
        tail_kernel,
        out_shape=[
            jax.ShapeDtypeStruct((R * C, F), BF),
            jax.ShapeDtypeStruct((PR * PC, F), BF),
        ],
        scratch_shapes=[
            pltpu.VMEM((20 * EC, F), BF),
            pltpu.VMEM((18 * EC, F), BF),
            pltpu.VMEM((PR * QC, F), F32),
        ],
        compiler_params=pltpu.CompilerParams(vmem_limit_bytes=8 << 20),
        name="tail",
    )(*in_hbm(terms), *on_chip(table), *in_hbm(grad), first_weights, second_weights)


def sum_at_owner(value, axes):
    tiles = lax.all_to_all(value.reshape(lax.axis_size(axes), -1, F), axes, 0, 0, tiled=True)
    return jnp.sum(tiles.astype(F32), axis=0).astype(BF)


def sent_to_all(value, axes):
    copies = jnp.broadcast_to(value, (lax.axis_size(axes), *value.shape))
    return lax.all_to_all(copies, axes, 0, 0, tiled=True)


def swapped(value):
    return lax.ppermute(value, "grp_1", [(0, 1), (1, 0)])


def total_of(keep, send):
    value = (keep.astype(F32) + swapped(send).astype(F32)).astype(BF)
    value = sum_at_owner(value, DEV)
    value = jnp.sum(sent_to_all(value, ("grp_0",)).astype(F32), axis=0).astype(BF)
    return sent_to_all(value, DEV).reshape(-1, F)


def clip_kernel(own_ref, other_ref, first_ref, second_ref):
    total = jnp.zeros((8, F), F32)
    for ref in (own_ref, other_ref):
        for n in range(3):
            part = ref[n * F : (n + 1) * F, :].astype(F32)
            total = total + jnp.sum((part * part).reshape(F // 8, 8, F), axis=0)
    square_sum = jnp.sum(jnp.sum(total, axis=1, keepdims=True), axis=0, keepdims=True)
    factor = jnp.minimum(1.0, 2.0 * F * lax.rsqrt(square_sum + 1e-06))
    is_first = lax.axis_index("grp_1") == 0
    for n in range(3):
        own = own_ref[n * F : (n + 1) * F, :].astype(F32) * factor
        other = other_ref[n * F : (n + 1) * F, :].astype(F32) * factor
        first_ref[n] = jnp.where(is_first, own, other)
        second_ref[n] = jnp.where(is_first, other, own)


def clipped(own, other):
    shape = jax.ShapeDtypeStruct((3, F, F), F32)
    return pl.pallas_call(
        clip_kernel,
        out_shape=[shape, shape],
        compiler_params=pltpu.CompilerParams(vmem_limit_bytes=8 << 20),
        name="clip",
    )(*on_chip(own, other))


def shards(pixels, offsets, first_weights, second_weights, cotangent):
    px = pixels.reshape(R * C, F)
    ct = cotangent.reshape(PR * PC, F)
    chip, cross, *strips, wide = row_messages(px, ct, offsets)
    cross = paired(cross, GRP, 1)
    chip = paired(chip, GRP, 0)
    first, second, rows = col_messages(*strips, wide, chip, cross)
    got = (paired(first, DEV, 0), paired(second, DEV, 1), rows)
    terms, keep, send, table, grad = main_stage(
        px, ct, wide, first_weights, second_weights, got
    )
    own = total_of(keep, send)
    grad_pixels, level = tail_stage(terms, table, grad, first_weights, second_weights)
    own, grad_pixels, level = lax.optimization_barrier((own, grad_pixels, level))
    first, second = clipped(own, swapped(own))
    return grad_pixels.reshape(R, C, F), first, second, level.reshape(PR, PC, F)


def solution(mesh):
    finer = Mesh(mesh.devices.reshape(-1, 2, 4, mesh.devices.shape[1] // 4), EVERY)
    in_specs = (P(GRP, DEV, None), P(GRP, DEV), P(), P(), P(GRP, DEV, None))
    out_specs = (P(GRP, DEV, None), P(), P(), P(GRP, DEV, None))
    return jax.shard_map(
        shards, mesh=finer, in_specs=in_specs, out_specs=out_specs, check_vma=False
    )
```

```python
import functools

import jax
import jax.numpy as jnp
from jax import lax
from jax.experimental import pallas as pl
from jax.experimental.pallas import tpu as pltpu
from jax.sharding import Mesh
from jax.sharding import PartitionSpec as P

GRP = ("grp_0", "grp_1")
DEV = ("dev_0", "dev_1")
EVERY = GRP + DEV
BF = jnp.bfloat16
F32 = jnp.float32

R, C, F = 16, 64, 256
PR, PC = R // 2, C // 2
HR, HC = 6, 8
ER, EC = R + 2 * HR, C + 2 * HC
QR, QC = PR + 6, PC + 8
OR = R + 16

STEPS = (
    (-1, 0, 1.0),
    (1, 0, 1.0),
    (0, -1, 1.0),
    (0, 1, 1.0),
    (-1, -1, 0.5),
    (-1, 1, 0.5),
    (1, -1, 0.5),
    (1, 1, 0.5),
)


def mm(a, b):
    return lax.dot_general(a, b, (((1,), (0,)), ((), ())), preferred_element_type=F32)


def mm_nt(a, b):
    return lax.dot_general(a, b, (((1,), (1,)), ((), ())), preferred_element_type=F32)


def mm_tn(a, b):
    return lax.dot_general(a, b, (((0,), (0,)), ((), ())), preferred_element_type=F32)


ROW_CT = HR * C
ROW_OFF = ROW_CT + 3 * PC
ROW_END = ROW_OFF + 16
COL_CT = ER * 6 + 8
COL_OFF = COL_CT + 64
COL_END = COL_OFF + OR // 2


def on_chip(*arrays):
    return [pltpu.with_memory_space_constraint(a, pltpu.VMEM) for a in arrays]


def in_hbm(*arrays):
    return [pltpu.with_memory_space_constraint(a, pltpu.HBM) for a in arrays]


def rolled(x, shift, axis):
    return pltpu.roll(x, shift % x.shape[axis], axis)


def in_parts(x):
    high = x.astype(BF).astype(F32)
    left = x - high
    middle = left.astype(BF).astype(F32)
    return high, middle, left - middle


def started(sems, pairs):
    copies = [pltpu.make_async_copy(src, dst, sems.at[n]) for n, (src, dst) in enumerate(pairs)]
    for copy in copies:
        copy.start()
    return copies


def row_pack_kernel(px_ref, ct_ref, px_rows, ct_rows, off_ref, *rest):
    up_ref, down_ref, pxl_ref, pxr_ref, ctl_ref, ctr_ref, wide, off_buf, sems = rest
    pairs = [(off_ref, off_buf)]
    for out, px_at, ct_at in ((up_ref, 0, 0), (down_ref, R - HR, PR - 3)):
        for ref, at, size, to in ((px_ref, px_at * C, HR * C, 0), (ct_ref, ct_at * PC, 3 * PC, ROW_CT)):
            pairs.append((ref.at[pl.ds(at, size), :], out.at[pl.ds(to, size), :]))
    pairs += [
        (px_rows.at[:, pl.ds(0, 16), :], pxl_ref),
        (px_rows.at[:, pl.ds(C - 16, 16), :], pxr_ref),
        (ct_rows.at[:, pl.ds(0, 16), :], ctl_ref),
        (ct_rows.at[:, pl.ds(PC - 16, 16), :], ctr_ref),
    ]
    copies = started(sems, pairs)
    wide[...] = jnp.zeros_like(wide)
    copies[0].wait()
    wide[:, 0:C] = off_buf[...]
    for out, off_at in ((up_ref, 0), (down_ref, R - 8)):
        high, middle, low = in_parts(wide[off_at : off_at + 8, :])
        packed = jnp.concatenate([high + rolled(middle, C, 1), low], 0)
        out[ROW_OFF:ROW_END, :] = jnp.concatenate([packed, jnp.zeros_like(packed)], 1).astype(BF)
    for copy in copies[1:]:
        copy.wait()


def row_messages(pixels, cotangent, offsets):
    return pl.pallas_call(
        row_pack_kernel,
        in_specs=[pl.BlockSpec(memory_space=pltpu.HBM)] * 5,
        out_shape=[
            pltpu.VMEM((ROW_END, F), BF),
            pltpu.VMEM((ROW_END, F), BF),
            pltpu.VMEM((R, 16, F), BF),
            pltpu.VMEM((R, 16, F), BF),
            pltpu.VMEM((PR, 16, F), BF),
            pltpu.VMEM((PR, 16, F), BF),
            pltpu.VMEM((R, 128), F32),
        ],
        scratch_shapes=[pltpu.VMEM((R, C), F32), pltpu.SemaphoreType.DMA((9,))],
        compiler_params=pltpu.CompilerParams(vmem_limit_bytes=4 << 20),
        name="row_pack",
    )(*in_hbm(pixels, cotangent, pixels.reshape(R, C, F), cotangent.reshape(PR, PC, F), offsets))


def row_offsets(ref):
    parts = ref[ROW_OFF:ROW_END, 0:128].astype(F32)
    whole = parts[0:8] + rolled(parts[0:8], C, 1) + parts[8:16]
    return jnp.where(lax.broadcasted_iota(jnp.int32, (8, 128), 1) < C, whole, 0.0)


def col_pack_kernel(*refs):
    pxl_ref, pxr_ref, ctl_ref, ctr_ref, off_ref, above_ref, below_ref, left_ref, right_ref, wide = refs
    wide[8 : 8 + R, :] = off_ref[...]
    wide[0:8, :] = row_offsets(above_ref)
    wide[8 + R : OR, :] = row_offsets(below_ref)
    lane = lax.broadcasted_iota(jnp.int32, (OR, 128), 1)
    row = lax.broadcasted_iota(jnp.int32, (8, F), 0)
    near = row < 4
    for out, px_ref, ct_ref, px_at, ct_at, half in (
        (left_ref, pxl_ref, ctl_ref, 0, 0, slice(0, 8)),
        (right_ref, pxr_ref, ctr_ref, C - 16, PC - 16, slice(8, 16)),
    ):

        def line(ref, k, base, width, at):
            if ref is above_ref or ref is below_ref:
                return ref[base + k * width + at : base + k * width + at + 16, :].astype(F32)[half]
            return ref[k].astype(F32)[half]

        lines = []
        for n, ref in ((HR, above_ref), (R, px_ref), (HR, below_ref)):
            for k in range(n):
                one = line(ref, k, 0, C, px_at)
                lines.append(one if out is left_ref else rolled(one, -2, 0))
        tiles = []
        for e in range(0, ER, 4):
            one, two, three, four = lines[e : e + 4]
            tiles.append(jnp.where(row < 6, one, rolled(two, 6, 0)))
            tiles.append(jnp.where(row < 4, rolled(two, -2, 0), rolled(three, 4, 0)))
            tiles.append(jnp.where(row < 2, rolled(three, -4, 0), rolled(four, 2, 0)))
        tiles.append(jnp.zeros((8, F), F32))
        for e in range(0, len(tiles), 2):
            out[e * 8 : e * 8 + 16, :] = jnp.concatenate(tiles[e : e + 2], 0).astype(BF)
        lines = []
        for n, ref in ((3, above_ref), (PR, ct_ref), (3, below_ref)):
            lines += [line(ref, k, ROW_CT, PC, ct_at) for k in range(n)]
        tiles = []
        for e in range(0, QR, 2):
            first, second = lines[e], lines[e + 1]
            if out is left_ref:
                second = rolled(second, 4, 0)
            else:
                first = rolled(first, 4, 0)
            tiles.append(jnp.where(near, first, second))
        tiles.append(jnp.zeros((8, F), F32))
        out[COL_CT:COL_OFF, :] = jnp.concatenate(tiles, 0).astype(BF)
        part = wide[...] if out is left_ref else rolled(wide[...], HC - C, 1)
        high, middle, low = in_parts(jnp.where(lane < HC, part, 0.0))
        packed = high + rolled(middle, HC, 1) + rolled(low, 2 * HC, 1)
        packed = packed[0 : OR // 2] + rolled(packed[OR // 2 :], 32, 1)
        out[COL_OFF:COL_END, :] = jnp.concatenate([packed, jnp.zeros_like(packed)], 1).astype(BF)


def col_messages(*parts):
    shape = pltpu.VMEM((COL_END, F), BF)
    return pl.pallas_call(
        col_pack_kernel,
        out_shape=[shape, shape],
        scratch_shapes=[pltpu.VMEM((OR, 128), F32)],
        compiler_params=pltpu.CompilerParams(vmem_limit_bytes=4 << 20),
        name="col_pack",
    )(*on_chip(*parts))


def exchanged(first, last, axis):
    count = lax.axis_size(axis)
    forward = [(i, i + 1) for i in range(count - 1)]
    backward = [(i + 1, i) for i in range(count - 1)]
    return lax.ppermute(last, axis, forward), lax.ppermute(first, axis, backward)


def inverse_roots(h, inside):
    degree = jnp.zeros_like(h)
    edges = {}
    for row_step, col_step, coupling in STEPS:
        other = rolled(rolled(h, row_step, 0), col_step, 1)
        present = rolled(rolled(inside, row_step, 0), col_step, 1)
        edges[row_step, col_step] = jnp.exp(-(h - other) * (h - other))
        degree = degree + coupling * present * edges[row_step, col_step]
    return lax.rsqrt(degree + 1.0 - inside) * inside, edges


def couplings(row_gap, col_gap):
    near = jnp.abs(col_gap)
    side = jnp.where(near == 0, 1.0, jnp.where(near == 1, 0.5, 0.0))
    own = jnp.where(near == 1, 1.0, 0.0)
    return jnp.where(row_gap == 0, own, jnp.where(jnp.abs(row_gap) == 1, side, 0.0))


def fine_windows(above, own, below):
    lane = lax.broadcasted_iota(jnp.int32, own.shape, 1)
    over = rolled(own, EC, 1)
    low = jnp.where(lane < EC, rolled(above, 1, 0), over)
    high = jnp.where(lane < 2 * EC - 128, over, rolled(rolled(below, -1, 0), 2 * EC - 128, 1))
    return jnp.concatenate([low, high], 1)


def pooled_windows(x):
    lane = lax.broadcasted_iota(jnp.int32, x.shape, 1)
    rows = [rolled(rolled(x, 1 - j, 0), QC * j, 1) for j in range(6)]
    low = jnp.where(
        lane < QC,
        rows[0],
        jnp.where(lane < 2 * QC, rows[1], jnp.where(lane < 3 * QC, rows[2], rows[3])),
    )
    high = jnp.where(
        lane < 4 * QC - 128,
        rows[3],
        jnp.where(
            lane < 5 * QC - 128, rows[4], jnp.where(lane < 6 * QC - 128, rows[5], 0.0)
        ),
    )
    return jnp.concatenate([low, high], 1)


def in_two(x):
    high = x.astype(BF)
    return jnp.concatenate([high, (x - high.astype(F32)).astype(BF)], 0)


def applied(table, values):
    both = mm(table, values)
    half = both.shape[0] // 2
    return both[0:half] + both[half:]


def transposed(x):
    if x.shape[0] < 128:
        x = jnp.concatenate([x, jnp.zeros((128 - x.shape[0], 128), F32)], 0)
    return x.T


def main_kernel(px_hbm, ct_hbm, w1_hbm, w2_hbm, off_ref, above_ref, below_ref, left_ref, right_ref, *rest):
    terms_hbm, keep_ref, send_ref, table_ref, grad_hbm = rest[:5]
    (h_ref, hw_ref, pick_ref, phw_ref, psw_ref, pxe_ref, f1_ref, f2_ref, f1c_ref, f2c_ref, slope_ref, hid_ref,
     poolf_ref, p1f_ref, p2f_ref, ctf_ref, ptab_ref, pb_ref, p1b_ref, ctb_ref, topb_ref,
     midf_ref, midb_ref, pgf_ref, sp_ref, agc_ref, halves_ref, px_ref, ct_ref, w1_ref, w2_ref,
     terms_ref, grad_ref, pxt_ref, f1t_ref, f2t_ref, strip_ref, sems, out_sems) = rest[5:]
    copies = started(
        sems, [(px_hbm, px_ref), (ct_hbm, ct_ref), (w1_hbm, w1_ref), (w2_hbm, w2_ref)]
    )
    core = lax.axis_index("grp_1")

    row0 = (lax.axis_index("grp_0") * 2 + lax.axis_index("grp_1")) * R
    col0 = (lax.axis_index("dev_0") * lax.axis_size("dev_1") + lax.axis_index("dev_1")) * C
    rows_all = lax.axis_size("grp_0") * lax.axis_size("grp_1") * R
    cols_all = lax.axis_size("dev_0") * lax.axis_size("dev_1") * C

    h_ref[8 : 8 + R, :] = off_ref[...]
    h_ref[0:8, :] = row_offsets(above_ref)
    h_ref[8 + R : OR, :] = row_offsets(below_ref)

    def col_offsets(ref):
        parts = ref[COL_OFF:COL_END, 0:128].astype(F32)
        parts = jnp.concatenate([parts, rolled(parts, -32, 1)], 0)
        whole = parts + rolled(parts, -HC, 1) + rolled(parts, -2 * HC, 1)
        return jnp.where(lax.broadcasted_iota(jnp.int32, (OR, 128), 1) < HC, whole, 0.0)

    h_ref[...] = (
        col_offsets(left_ref) + rolled(h_ref[...], HC, 1) + rolled(col_offsets(right_ref), HC + C, 1)
    )
    h = h_ref[...]
    q = lax.broadcasted_iota(jnp.int32, (OR, 128), 0)
    c = lax.broadcasted_iota(jnp.int32, (OR, 128), 1)
    row_id = row0 - 8 + q
    col_id = col0 - HC + c
    inside = (
        (row_id >= 0) & (row_id < rows_all) & (col_id >= 0) & (col_id < cols_all) & (c < EC)
    ).astype(F32)
    s, edges = inverse_roots(h, inside)

    pick_r = lax.broadcasted_iota(jnp.int32, (OR // 2, OR), 1) // 2
    pick_r = jnp.where(pick_r == lax.broadcasted_iota(jnp.int32, (OR // 2, OR), 0), 0.5, 0.0)
    pick_c = lax.broadcasted_iota(jnp.int32, (128, 128), 0) // 2
    pick_c = jnp.where(pick_c == lax.broadcasted_iota(jnp.int32, (128, 128), 1), 0.5, 0.0)
    ph = jnp.dot(pick_r, h, precision=lax.Precision.HIGHEST, preferred_element_type=F32)
    ph = jnp.dot(ph, pick_c, precision=lax.Precision.HIGHEST, preferred_element_type=F32)
    pq = lax.broadcasted_iota(jnp.int32, (OR // 2, 128), 0)
    pc = lax.broadcasted_iota(jnp.int32, (OR // 2, 128), 1)
    prow = row0 // 2 - 4 + pq
    pcol = col0 // 2 - 4 + pc
    pinside = (
        (prow >= 0) & (prow < rows_all // 2) & (pcol >= 0) & (pcol < cols_all // 2) & (pc < QC)
    ).astype(F32)
    ps, _ = inverse_roots(ph, pinside)

    k = lax.broadcasted_iota(jnp.int32, (EC, 256), 1)
    i = lax.broadcasted_iota(jnp.int32, (EC, 256), 0)
    block = (k >= EC).astype(jnp.int32) + (k >= 2 * EC).astype(jnp.int32)
    gap = jnp.where(k < 3 * EC, k - block * EC - i, 9)
    for n, col_step in enumerate((-1, 0, 1)):
        parts = []
        for row_step in (-1, 0, 1):
            if (row_step, col_step) == (0, 0):
                parts.append(jnp.zeros_like(h))
                continue
            coupling = 0.5 if row_step and col_step else 1.0
            other = rolled(rolled(s, row_step, 0), col_step, 1)
            parts.append(-coupling * edges[row_step, col_step] * (s * other))
        window = fine_windows(*parts)
        high = window.astype(BF).astype(F32)
        hw_ref[n] = high
        hw_ref[3 + n] = window - high
        pick_ref[n] = jnp.where(gap == col_step, 1.0, 0.0).astype(BF)
    for r in range(1, ER - 1):
        at = r + 2
        for part in (0, 1):
            lines = []
            for n in range(3):
                line = hw_ref[3 * part + n, at : at + 1, :]
                lines.append(jnp.broadcast_to(line, (16, 256)).astype(BF))
            base = (2 * (r - 1) + part) * EC
            for t in range(0, EC, 16):
                picked = pick_ref[0, t : t + 16, :] * lines[0]
                picked = picked + pick_ref[1, t : t + 16, :] * lines[1]
                picked = picked + pick_ref[2, t : t + 16, :] * lines[2]
                table_ref[base + t : base + t + 16, :] = picked
    phw_ref[...] = pooled_windows(ph)
    psw_ref[...] = pooled_windows(ps)
    pht, pst = transposed(ph), transposed(ps)
    k = lax.broadcasted_iota(jnp.int32, (QC, 256), 1)
    i = lax.broadcasted_iota(jnp.int32, (QC, 256), 0)
    block = sum((k >= QC * j).astype(jnp.int32) for j in range(1, 6))
    plinks = [-couplings(block - 1 - j, k - block * QC - i) for j in range(4)]
    for b in range(3):
        at = 2 + 4 * b
        for j in (0, 2):
            both = []
            for jj in (j, j + 1):
                col = at + jj
                gap = pht[0:QC, col : col + 1] - phw_ref[at : at + 1, :]
                scale = pst[0:QC, col : col + 1] * psw_ref[at : at + 1, :]
                both.append(plinks[jj] * jnp.exp(-gap * gap) * scale)
            two = in_two(jnp.concatenate(both, 0))
            at_row = 2 * b * 160 + j * QC
            ptab_ref[at_row : at_row + 2 * QC, :] = two[0 : 2 * QC]
            ptab_ref[at_row + 160 : at_row + 160 + 2 * QC, :] = two[2 * QC :]

    copies[0].wait()
    copies[1].wait()
    for n, ref in enumerate((left_ref, right_ref)):
        strip_ref[n, 0:8, :] = jnp.zeros((8, F), F32)
        strip_ref[n, 8 : 8 + COL_CT, :] = ref[0:COL_CT, :].astype(F32)
    for at, n, ref in ((0, HR, above_ref), (HR, R, px_ref), (HR + R, HR, below_ref)):
        for r in range(0, n, 2):
            middle = ref[r * C : (r + 2) * C, :].astype(F32)
            lines = []
            for k in (0, 1):
                e = 8 + (at + r + k) * 6
                lines.append(strip_ref[0, e - 2 : e + 6, :])
                lines.append(middle[k * C : (k + 1) * C])
                lines.append(strip_ref[1, e : e + 8, :])
            row = (at + r) * EC
            pxe_ref[row : row + 2 * EC, :] = jnp.concatenate(lines, 0).astype(BF)

    left = left_ref[COL_CT:COL_OFF, :].astype(F32)
    right = right_ref[COL_CT:COL_OFF, :].astype(F32)
    for at, n, base, ref in ((0, 3, ROW_CT, above_ref), (3, PR, 0, ct_ref), (3 + PR, 3, ROW_CT, below_ref)):
        for r in range(n):
            e = at + r
            ctf_ref[e * QC : e * QC + 4, :] = left[e * 4 : e * 4 + 4]
            ctf_ref[e * QC + 4 : e * QC + 4 + PC, :] = ref[base + r * PC : base + (r + 1) * PC, :].astype(F32)
            ctf_ref[e * QC + 4 + PC : (e + 1) * QC, :] = right[e * 4 : e * 4 + 4]
    ctb_ref[...] = ctf_ref[...].astype(BF)

    copies[2].wait()
    copies[3].wait()

    def table_of(r):
        return table_ref[2 * (r - 1) * EC : 2 * r * EC, 0 : 3 * EC]

    def turn(ref, to_ref, n):
        to_ref[:, n * 128 : (n + 1) * 128] = ref[n * 128 : (n + 1) * 128, :].T

    for r in range(1, ER - 1):
        if 4 <= r < 20 and r % 2 == 0:
            turn(px_ref, pxt_ref, (r - 4) // 2)
        one = applied(table_of(r), pxe_ref[(r - 1) * EC : (r + 2) * EC, :])
        f1_ref[(r - 1) * EC : r * EC, :] = one.astype(BF)
        if HR <= r < HR + R:
            f1c_ref[(r - HR) * C : (r - HR + 1) * C, :] = one[HC : HC + C].astype(BF)
    for r in range(2, ER - 2):
        if 4 <= r < 20 and r % 2 == 0:
            turn(f1c_ref, f1t_ref, (r - 4) // 2)
        two = 2.0 * applied(table_of(r), f1_ref[(r - 2) * EC : (r + 1) * EC, :])
        two = two - pxe_ref[r * EC : (r + 1) * EC, :].astype(F32)
        f2_ref[(r - 2) * EC : (r - 1) * EC, :] = two.astype(BF)
        if HR <= r < HR + R:
            f2c_ref[(r - HR) * C : (r - HR + 1) * C, :] = two[HC : HC + C].astype(BF)
    poolf_ref[...] = jnp.zeros_like(poolf_ref)
    p1f_ref[...] = jnp.zeros_like(p1f_ref)
    midf_ref[...] = jnp.zeros_like(midf_ref)
    for b in range(6):
        r = 2 + 4 * b
        terms = [
            pxe_ref[r * EC : (r + 4) * EC, :],
            f1_ref[(r - 1) * EC : (r + 3) * EC, :],
            f2_ref[(r - 2) * EC : (r + 2) * EC, :],
        ]
        act = mm(jnp.concatenate(terms, 1), w1_ref[...].reshape(3 * F, F))
        sig = 0.5 * jnp.tanh(0.5 * act) + 0.5
        hid = act * sig
        slope_ref[(r - 2) * EC : (r + 2) * EC, :] = sig + hid * (1.0 - sig)
        for n in ((0, 1), (2, 3), (4,), (5,), (6,), (7,))[b]:
            turn(f2c_ref, f2t_ref, n)
        for n in (0, 1):
            half = hid[:, n * 128 : (n + 1) * 128]
            ref = hid_ref.at[2 * b + n]
            ref[0:EC, :] = half[0:EC] + half[EC : 2 * EC]
            ref[EC : 2 * EC, :] = half[2 * EC : 3 * EC] + half[3 * EC : 4 * EC]
            pooled = 0.25 * (ref[pl.ds(0, EC, stride=2), :] + ref[pl.ds(1, EC, stride=2), :])
            pooled = pooled.astype(BF).astype(F32)
            poolf_ref[(1 + 2 * b) * QC : (3 + 2 * b) * QC, n * 128 : (n + 1) * 128] = pooled
    pb_ref[...] = poolf_ref[...].astype(BF)

    def ptable_of(b):
        return ptab_ref[b * 320 : (b + 1) * 320, 0 : 6 * QC]

    for b in range(3):
        one = applied(ptable_of(b), pb_ref[b * 160 : b * 160 + 6 * QC, :])
        p1f_ref[(1 + 4 * b) * QC : (5 + 4 * b) * QC, :] = one
    p1b_ref[...] = p1f_ref[...].astype(BF)
    for b in range(3):
        two = 2.0 * applied(ptable_of(b), p1b_ref[b * 160 : b * 160 + 6 * QC, :])
        lines = slice((1 + 4 * b) * QC, (5 + 4 * b) * QC)
        p2f_ref[lines, :] = two - poolf_ref[lines, :]
    own = slice(3 * QC, 11 * QC)
    terms = [poolf_ref[own, :].astype(BF), p1f_ref[own, :].astype(BF), p2f_ref[own, :].astype(BF)]
    for n, term in enumerate(terms):
        terms_ref[n] = term
    outward = [pltpu.make_async_copy(terms_ref, terms_hbm, out_sems.at[0])]
    outward[0].start()
    col = lax.broadcasted_iota(jnp.int32, (QC, F), 0)
    keep = ((col >= 4) & (col < 4 + PC)).astype(F32)
    cot_own = (ctf_ref[own, :].reshape(PR, QC, F) * keep[None]).reshape(PR * QC, F).astype(BF)
    for n, term in enumerate(terms):
        halves_ref[1 - core, n * F : (n + 1) * F, :] = mm_tn(term, cot_own).astype(BF)

    cot = ctb_ref[...]
    topb_ref[...] = mm_nt(cot, w2_ref[2]).astype(BF)
    from_one = mm_nt(cot, w2_ref[1])
    for b in range(3):
        lines = slice((1 + 4 * b) * QC, (5 + 4 * b) * QC)
        mid = 2.0 * applied(ptable_of(b), topb_ref[b * 160 : b * 160 + 6 * QC, :])
        midf_ref[lines, :] = from_one[lines] + mid
    midb_ref[...] = midf_ref[...].astype(BF)
    from_zero = mm_nt(cot, w2_ref[0]) - topb_ref[...].astype(F32)
    for b in range(3):
        lines = slice((1 + 4 * b) * QC, (5 + 4 * b) * QC)
        pgf_ref[lines, :] = from_zero[lines] + applied(ptable_of(b), midb_ref[b * 160 : b * 160 + 6 * QC, :])
    for b in range(5):
        u = 2 + 2 * b
        grad = 0.25 * pgf_ref[u * QC : (u + 2) * QC, :]
        for n in (0, 1):
            ref = sp_ref.at[2 * b + n]
            ref[pl.ds(0, 2 * QC, stride=2), :] = grad[:, n * 128 : (n + 1) * 128]
            ref[pl.ds(1, 2 * QC, stride=2), :] = grad[:, n * 128 : (n + 1) * 128]
        for n in range(4):
            r = 2 * u + n
            lines = slice((n // 2) * EC, (n // 2 + 1) * EC)
            spread = jnp.concatenate([sp_ref[2 * b, lines, :], sp_ref[2 * b + 1, lines, :]], 1)
            grad_row = spread * slope_ref[(r - 2) * EC : (r - 1) * EC, :]
            grad_ref[(r - 4) * EC : (r - 3) * EC, :] = grad_row.astype(BF)
            if HR <= r < HR + R:
                agc_ref[(r - HR) * C : (r - HR + 1) * C, :] = grad_row[HC : HC + C].astype(BF)
    outward.append(pltpu.make_async_copy(grad_ref, grad_hbm, out_sems.at[1]))
    outward[1].start()
    for n, ref in enumerate((pxt_ref, f1t_ref, f2t_ref)):
        halves_ref[core, n * F : (n + 1) * F, :] = mm(ref[...], agc_ref[...]).astype(BF)
    keep_ref[...] = halves_ref[0]
    send_ref[...] = halves_ref[1]
    for copy in outward:
        copy.wait()


def main_stage(pixels, cotangent, offsets, first_weights, second_weights, got):
    fine, pooled = ER * EC, QR * QC
    scratch = [
        ((OR, 128), F32),
        ((6, OR, 256), F32),
        ((3, EC, 256), BF),
        ((OR // 2, 256), F32),
        ((OR // 2, 256), F32),
        ((fine, F), BF),
        ((26 * EC, F), BF),
        ((24 * EC, F), BF),
        ((R * C, F), BF),
        ((R * C, F), BF),
        ((24 * EC, F), F32),
        ((12, 2 * EC, 128), F32),
        ((pooled, F), F32),
        ((pooled, F), F32),
        ((pooled, F), F32),
        ((pooled, F), F32),
        ((960, 256), BF),
        ((pooled, F), BF),
        ((pooled, F), BF),
        ((pooled, F), BF),
        ((pooled, F), BF),
        ((pooled, F), F32),
        ((pooled, F), BF),
        ((pooled, F), F32),
        ((10, 2 * EC, 128), F32),
        ((R * C, F), BF),
        ((2, 3 * F, F), BF),
        ((R * C, F), BF),
        ((PR * PC, F), BF),
        ((3, F, F), BF),
        ((3, F, F), BF),
        ((3, PR * QC, F), BF),
        ((20 * EC, F), BF),
        ((F, R * C), BF),
        ((F, R * C), BF),
        ((F, R * C), BF),
        ((2, 8 + COL_CT, F), F32),
    ]
    return pl.pallas_call(
        main_kernel,
        out_shape=[
            pltpu.HBM((3, PR * QC, F), BF),
            pltpu.VMEM((3 * F, F), BF),
            pltpu.VMEM((3 * F, F), BF),
            pltpu.VMEM((52 * EC, 256), BF),
            pltpu.HBM((20 * EC, F), BF),
        ],
        in_specs=[pl.BlockSpec(memory_space=pl.ANY)] * 4
        + [pl.BlockSpec(memory_space=pltpu.VMEM)] * 5,
        scratch_shapes=[pltpu.VMEM(shape, dtype) for shape, dtype in scratch]
        + [pltpu.SemaphoreType.DMA((4,)), pltpu.SemaphoreType.DMA((2,))],
        compiler_params=pltpu.CompilerParams(vmem_limit_bytes=20 << 20),
        name="main",
    )(pixels, cotangent, first_weights, second_weights, *on_chip(offsets, *got))


def tail_kernel(terms_ref, table_ref, grad_ref, w_ref, w2_ref, out_ref, level_ref, top_ref, mid_ref, low_ref):
    top_ref[...] = mm_nt(grad_ref[...], w_ref[2]).astype(BF)
    for b in range(9):
        r = 5 + 2 * b
        base = mm_nt(grad_ref[(r - 4) * EC : (r - 2) * EC, :], w_ref[1])
        for n in (0, 1):
            table = table_ref[2 * (r + n - 1) * EC : 2 * (r + n) * EC, 0 : 3 * EC]
            mid = 2.0 * applied(table, top_ref[(r + n - 5) * EC : (r + n - 2) * EC, :])
            mid = base[n * EC : (n + 1) * EC] + mid
            mid_ref[(r + n - 5) * EC : (r + n - 4) * EC, :] = mid.astype(BF)
    for b in range(8):
        r = 6 + 2 * b
        base = mm_nt(grad_ref[(r - 4) * EC : (r - 2) * EC, :], w_ref[0])
        base = base - top_ref[(r - 4) * EC : (r - 2) * EC, :].astype(F32)
        for n in (0, 1):
            table = table_ref[2 * (r + n - 1) * EC : 2 * (r + n) * EC, 0 : 3 * EC]
            line = base[n * EC : (n + 1) * EC] + applied(table, mid_ref[(r + n - 6) * EC : (r + n - 3) * EC, :])
            at = (r + n - HR) * C
            out_ref[at : at + C, :] = line[HC : HC + C].astype(BF)
    low_ref[...] = sum(mm(terms_ref[n], w2_ref[n]) for n in range(3))
    for r in range(PR):
        level_ref[r * PC : (r + 1) * PC, :] = low_ref[r * QC + 4 : r * QC + 4 + PC, :].astype(BF)


def tail_stage(terms, table, grad, first_weights, second_weights):
    return pl.pallas_call(
        tail_kernel,
        out_shape=[
            jax.ShapeDtypeStruct((R * C, F), BF),
            jax.ShapeDtypeStruct((PR * PC, F), BF),
        ],
        scratch_shapes=[
            pltpu.VMEM((20 * EC, F), BF),
            pltpu.VMEM((18 * EC, F), BF),
            pltpu.VMEM((PR * QC, F), F32),
        ],
        compiler_params=pltpu.CompilerParams(vmem_limit_bytes=8 << 20),
        name="tail",
    )(*in_hbm(terms), *on_chip(table), *in_hbm(grad), first_weights, second_weights)


def sum_at_owner(value, axes):
    tiles = lax.all_to_all(value.reshape(lax.axis_size(axes), -1, F), axes, 0, 0, tiled=True)
    return jnp.sum(tiles.astype(F32), axis=0).astype(BF)


def sent_to_all(value, axes):
    copies = jnp.broadcast_to(value, (lax.axis_size(axes), *value.shape))
    return lax.all_to_all(copies, axes, 0, 0, tiled=True)


def swapped(value):
    return lax.ppermute(value, "grp_1", [(0, 1), (1, 0)])


def total_of(keep, send):
    value = (keep.astype(F32) + swapped(send).astype(F32)).astype(BF)
    value = sum_at_owner(value, DEV)
    value = jnp.sum(sent_to_all(value, ("grp_0",)).astype(F32), axis=0).astype(BF)
    return sent_to_all(value, DEV).reshape(-1, F)


def clip_kernel(own_ref, other_ref, first_ref, second_ref):
    total = jnp.zeros((8, F), F32)
    for ref in (own_ref, other_ref):
        for n in range(3):
            part = ref[n * F : (n + 1) * F, :].astype(F32)
            total = total + jnp.sum((part * part).reshape(F // 8, 8, F), axis=0)
    square_sum = jnp.sum(jnp.sum(total, axis=1, keepdims=True), axis=0, keepdims=True)
    factor = jnp.minimum(1.0, 2.0 * F * lax.rsqrt(square_sum + 1e-06))
    is_first = lax.axis_index("grp_1") == 0
    for n in range(3):
        own = own_ref[n * F : (n + 1) * F, :].astype(F32) * factor
        other = other_ref[n * F : (n + 1) * F, :].astype(F32) * factor
        first_ref[n] = jnp.where(is_first, own, other)
        second_ref[n] = jnp.where(is_first, other, own)


def clipped(own, other):
    shape = jax.ShapeDtypeStruct((3, F, F), F32)
    return pl.pallas_call(
        clip_kernel,
        out_shape=[shape, shape],
        compiler_params=pltpu.CompilerParams(vmem_limit_bytes=8 << 20),
        name="clip",
    )(*on_chip(own, other))


def shards(pixels, offsets, first_weights, second_weights, cotangent):
    px = pixels.reshape(R * C, F)
    ct = cotangent.reshape(PR * PC, F)
    up, down, *strips, wide = row_messages(px, ct, offsets)
    above, below = exchanged(up, down, GRP)
    left, right = exchanged(*col_messages(*strips, wide, above, below), DEV)
    got = (above, below, left, right)
    terms, keep, send, table, grad = main_stage(
        px, ct, wide, first_weights, second_weights, got
    )
    own = total_of(keep, send)
    grad_pixels, level = tail_stage(terms, table, grad, first_weights, second_weights)
    own, grad_pixels, level = lax.optimization_barrier((own, grad_pixels, level))
    first, second = clipped(own, swapped(own))
    return grad_pixels.reshape(R, C, F), first, second, level.reshape(PR, PC, F)


def solution(mesh):
    finer = Mesh(mesh.devices.reshape(-1, 2, 4, mesh.devices.shape[1] // 4), EVERY)
    in_specs = (P(GRP, DEV, None), P(GRP, DEV), P(), P(), P(GRP, DEV, None))
    out_specs = (P(GRP, DEV, None), P(), P(), P(GRP, DEV, None))
    return jax.shard_map(
        shards, mesh=finer, in_specs=in_specs, out_specs=out_specs, check_vma=False
    )
```
